32 devices in a mesh: tm: 8 (over z, x), space: 4 (over y, core).
Axes of the slice: x: 2, y: 2, z: 4, core: 2. Of those that a mesh axis runs over, the one named last changes fastest.
Arguments:
- video: bfloat16 [16, 32, 32, 384], P('tm', 'space'), may hold values from -6 to 6
- conv_weight: bfloat16 [3, 3, 3, 384, 384], replicated, may hold values from -0.0625 to 0.0625
- embed_weight: bfloat16 [384, 1152], replicated, may hold values from -0.3125 to 0.3125
- q_weight: bfloat16 [1152, 1152], replicated, may hold values from -0.1875 to 0.1875
- k_weight: bfloat16 [1152, 1152], replicated, may hold values from -0.1875 to 0.1875
- v_weight: bfloat16 [1152, 1152], replicated, may hold values from -0.1875 to 0.1875
- initial_state: float32 [16, 72, 72], P('space'), may hold values from -1536 to 1536
- probe_in: int32 [16, 32, 32, 1152], P('tm', 'space'), may hold values from -1 to 1, as said below
- probe_out: int32 [16, 32, 32, 1152], P('tm', None, None, 'space'), may hold values from -1 to 1, as said below
Outputs:
- flow: bfloat16 [16, 32, 32, 1152], P('tm', None, None, 'space')
- tangent: bfloat16 [16, 32, 32, 1152], P('tm', None, None, 'space')
- adjoint: bfloat16 [16, 32, 32, 1152], P('tm', 'space')
- state_cotangent: float32 [64, 16, 72, 72], P('tm', 'space')
The draws below stay inside these ranges and needn't reach their ends.
Inputs may be any that keep to these rules, and one draw needn't show every extreme that they name: `probe_in`: every entry is -1 or +1. `probe_out`: every entry is -1 or +1.
All inputs are finite; a program needn't handle non-finite values.
Results may differ from the reference program's by a relative error of at most 0.012.
Values may be sent and summed in bfloat16 or wider, within the bound.
No kernel may reach another device: no remote copies, remote signals or barrier semaphores. Data moves between devices by JAX's collectives and lax.ppermute only.
A program may use at most 128 MiB of HBM per device.

```python
import jax
import jax.numpy as jnp
from jax import lax

C = 384
D = 1152
HEADS = 16
SPAN = 256
FRAME_H = 32
FRAME_W = 32
FRAMES = 16
HEAD_DIM = 72


def draw_probe_in(key, part):
    coins = jax.random.randint(jax.random.fold_in(key, 101), (FRAMES, FRAME_H, FRAME_W, D), 0, 2, dtype=jnp.int32)
    return 2 * coins - 1


def draw_probe_out(key, part):
    coins = jax.random.randint(jax.random.fold_in(key, 202), (FRAMES, FRAME_H, FRAME_W, D), 0, 2, dtype=jnp.int32)
    return 2 * coins - 1


def level_of(stream_key, extent, cuts, low, high):
    level = 1.0
    for axis_at, blocks in cuts:
        draws = jax.random.uniform(jax.random.fold_in(jax.random.fold_in(stream_key, 6), axis_at), (blocks,), jnp.float32, low / len(cuts), high / len(cuts))
        level = level * jnp.repeat(jnp.exp(draws), extent[axis_at] // blocks).reshape((-1,) + (1,) * (len(extent) - 1 - axis_at))
    return level


def noise(rng, shape, width, bound, shards=(), held_as=jnp.bfloat16):
    factor_of = level_of(rng, shape, shards, -0.22, 0.18) if shards else 1.0
    entries = jax.random.normal(rng, shape, jnp.float32) * width * factor_of
    return jnp.minimum(jnp.maximum(entries, -bound), bound).astype(held_as)


def setup_inputs(seed: int = 0) -> dict:
    seeds = jax.random.split(jax.random.key(seed), 10)
    return {
        "video": noise(seeds[0], (FRAMES, FRAME_H, FRAME_W, C), 1.0, 6.0, ((0, 8), (1, 4))),
        "conv_weight": noise(seeds[1], (3, 3, 3, C, C), (27 * C) ** -0.5, 0.0625),
        "embed_weight": noise(seeds[2], (C, D), C ** -0.5, 0.3125),
        "q_weight": noise(seeds[3], (D, D), D ** -0.5, 0.1875),
        "k_weight": noise(seeds[4], (D, D), D ** -0.5, 0.1875),
        "v_weight": noise(seeds[5], (D, D), D ** -0.5, 0.1875),
        "initial_state": noise(seeds[6], (HEADS, HEAD_DIM, HEAD_DIM), (0.015 * FRAMES * FRAME_H * FRAME_W), 1536.0, ((0, 4),), jnp.float32),
        "probe_in": draw_probe_in(jax.random.fold_in(seeds[9], 71), 0),
        "probe_out": draw_probe_out(jax.random.fold_in(seeds[9], 71), 0),
    }


def flat_dot(operand, matrix):
    dims_in = operand.shape
    result = jnp.dot(operand.reshape(-1, dims_in[-1]), matrix, preferred_element_type=jnp.float32)
    return result.reshape(dims_in[:-1] + (matrix.shape[1],))

def product(form, first, second):
    return jnp.einsum(form, first.astype(jnp.float32), second.astype(jnp.float32), precision=lax.Precision.HIGHEST)

def encode(video, conv_weight, embed_weight):
    padded = jnp.pad(video, ((2, 0), (1, 1), (1, 1), (0, 0)))
    frames, height, columns = (video.shape[0], video.shape[1], video.shape[2])
    summed = jnp.zeros((frames, height, columns, conv_weight.shape[4]), jnp.float32)
    for tap_time in range(3):
        for tap_row in range(3):
            for tap_col in range(3):
                window = padded[tap_time:tap_time + frames, tap_row:tap_row + height, tap_col:tap_col + columns]
                summed = summed + flat_dot(window, conv_weight[tap_time, tap_row, tap_col])
    active = jax.nn.silu(summed).astype(jnp.bfloat16)
    return flat_dot(active, embed_weight).astype(jnp.bfloat16)

def reference(video, conv_weight, embed_weight, q_weight, k_weight, v_weight, initial_state, probe_in, probe_out):
    latent = encode(video, conv_weight, embed_weight)
    direction = probe_in.astype(jnp.bfloat16)
    blocks = FRAMES * FRAME_H * FRAME_W // SPAN

    def split(array):
        return array.reshape(blocks, SPAN, HEADS, D // HEADS)
    query_rows = split(flat_dot(latent, q_weight).astype(jnp.bfloat16))
    key_rows = split(flat_dot(latent, k_weight).astype(jnp.bfloat16))
    value_rows = split(flat_dot(latent, v_weight).astype(jnp.bfloat16))
    query_dot = split(flat_dot(direction, q_weight).astype(jnp.bfloat16))
    key_dot = split(flat_dot(direction, k_weight).astype(jnp.bfloat16))
    value_dot = split(flat_dot(direction, v_weight).astype(jnp.bfloat16))
    states = product('cthd,cthe->chde', key_rows, value_rows)
    state_dot = product('cthd,cthe->chde', key_dot, value_rows) + product('cthd,cthe->chde', key_rows, value_dot)
    prefix = initial_state[None] + jnp.cumsum(states, 0)
    prefix_dot = jnp.cumsum(state_dot, 0)
    mixed = product('cthd,chde->cthe', query_rows, prefix)
    mixed_dot = product('cthd,chde->cthe', query_dot, prefix) + product('cthd,chde->cthe', query_rows, prefix_dot)
    scale_inv = lax.rsqrt(lax.optimization_barrier(jnp.mean(mixed * mixed, -1, keepdims=True)) + 1e-06)
    cubed = scale_inv * scale_inv * scale_inv
    flow = (mixed * scale_inv).astype(jnp.bfloat16)
    along = lax.optimization_barrier(jnp.mean(mixed * mixed_dot, -1, keepdims=True))
    tangent = (mixed_dot * scale_inv - mixed * cubed * along).astype(jnp.bfloat16)
    cotangent = split(probe_out.astype(jnp.float32))
    across = lax.optimization_barrier(jnp.mean(mixed * cotangent, -1, keepdims=True))
    mixed_bar = cotangent * scale_inv - mixed * cubed * across
    query_bar = product('cthe,chde->cthd', mixed_bar, prefix).astype(jnp.bfloat16)
    prefix_bar = product('cthd,cthe->chde', query_rows, mixed_bar)
    state_bar = jnp.cumsum(prefix_bar[::-1], 0)[::-1]
    key_bar = product('cthe,chde->cthd', value_rows, state_bar).astype(jnp.bfloat16)
    value_bar = product('cthd,chde->cthe', key_rows, state_bar).astype(jnp.bfloat16)
    full_shape = (FRAMES, FRAME_H, FRAME_W, D)
    summed = flat_dot(query_bar.reshape(full_shape), q_weight.T)
    summed = summed + flat_dot(key_bar.reshape(full_shape), k_weight.T)
    summed = summed + flat_dot(value_bar.reshape(full_shape), v_weight.T)
    return (flow.reshape(full_shape), tangent.reshape(full_shape), summed.astype(jnp.bfloat16), state_bar)
```

```python
import functools

import jax
import jax.numpy as jnp
from jax import lax
from jax.experimental import pallas as pl
from jax.experimental.pallas import tpu as pltpu
from jax.sharding import PartitionSpec as P

D = 1152
HEADS = 16
SPAN = 256
HEAD = D // HEADS
PAIR = 2 * HEAD
F32 = jnp.float32
BF16 = jnp.bfloat16
VMEM_BYTES = 56 * 1024 * 1024


def call(body, name, grid, ins, outs, args, scratch=(), flops=0, moved=0):
    return pl.pallas_call(
        body,
        name=name,
        grid=grid,
        in_specs=ins,
        out_specs=[spec for spec, _ in outs],
        out_shape=[shape for _, shape in outs],
        scratch_shapes=list(scratch),
        compiler_params=pltpu.CompilerParams(vmem_limit_bytes=VMEM_BYTES),
        cost_estimate=pl.CostEstimate(flops=flops, bytes_accessed=moved, transcendentals=0),
    )(*args)


def whole(array, steps):
    zeros = (0,) * array.ndim
    return pl.BlockSpec(array.shape, lambda *_: zeros)


def struct(shape, dtype):
    return jax.ShapeDtypeStruct(shape, dtype)


def dot(a, b):
    return jnp.dot(a, b, preferred_element_type=F32)


def dot_nt(a, b):
    return lax.dot_general(a, b, (((1,), (1,)), ((), ())), preferred_element_type=F32)


def dot_tn(a, b):
    return lax.dot_general(a, b, (((0,), (0,)), ((), ())), preferred_element_type=F32)


def same_head():
    row = lax.broadcasted_iota(jnp.int32, (PAIR, PAIR), 0) < HEAD
    col = lax.broadcasted_iota(jnp.int32, (PAIR, PAIR), 1) < HEAD
    return row == col


def spread(packed):
    both = jnp.concatenate([packed, packed], 0)
    return jnp.where(same_head(), both, 0.0).astype(BF16)


def packed_of(square):
    col = lax.broadcasted_iota(jnp.int32, (HEAD, PAIR), 1) < HEAD
    return jnp.where(col, square[:HEAD], square[HEAD:])


def probe_body(groups, share, x_ref, q_ref, k_ref, v_ref, qd_ref, kd_ref, vd_ref):
    x = x_ref[...].astype(F32).astype(BF16)
    query = dot(x, q_ref[...])
    for g in range(groups):
        qd_ref[g] = query[:, g * share : (g + 1) * share].astype(BF16)
    kd_ref[...] = dot(x, k_ref[...]).astype(BF16)
    vd_ref[...] = dot(x, v_ref[...]).astype(BF16)


def query_body(groups, share, x_ref, q_ref, out_ref):
    query = dot(x_ref[...], q_ref[...])
    for g in range(groups):
        out_ref[g] = query[:, g * share : (g + 1) * share].astype(BF16)


def conv_body(
    own_ref, up_ref, down_ref, prev_ref, prev_up_ref, prev_down_ref, w_ref, embed_ref,
    out_ref, wide, total,
):
    tap = pl.program_id(0)
    frames, tile_rows, columns, channels = own_ref.shape
    tokens = tile_rows * columns

    @pl.when(tap == 0)
    def _():
        total[...] = jnp.zeros_like(total)
        span = (tile_rows + 2) * columns
        column = lax.broadcasted_iota(jnp.int32, (span, channels), 0) % columns
        for f in range(2 * frames):
            refs = (prev_ref, prev_up_ref, prev_down_ref) if f < frames else (own_ref, up_ref, down_ref)
            mid, top, bottom = (r[f % frames].reshape(-1, channels) for r in refs)
            x = jnp.concatenate([top, mid, bottom], 0).astype(F32)
            left = jnp.where(column == 0, 0.0, pltpu.roll(x, 1, 0))
            right = jnp.where(column == columns - 1, 0.0, pltpu.roll(x, span - 1, 0))
            wide[f, :, :channels] = left.astype(BF16)
            wide[f, :, channels : 2 * channels] = x.astype(BF16)
            wide[f, :, 2 * channels :] = right.astype(BF16)

    tap_time, tap_row = tap // 3, tap % 3
    rows = pl.ds(pl.multiple_of(tap_row * columns, columns), tokens)
    window = jnp.concatenate([wide[tap_time + f, rows, :] for f in range(frames)], 0)
    total[...] += dot(window, w_ref[0, 0])

    @pl.when(tap == 8)
    def _():
        u = total[...]
        active = (u / (1.0 + jnp.exp(-u))).astype(BF16)
        out_ref[...] = dot(active, embed_ref[...]).astype(BF16)


def state_body(x_ref, k_ref, v_ref, kd_ref, vd_ref, key_ref, value_ref, state_ref):
    x = x_ref[...]
    key = dot(x, k_ref[...]).astype(BF16)
    key_ref[...] = key
    value = dot(x, v_ref[...]).astype(BF16)
    value_ref[...] = value
    for p in range(HEADS // 2):
        at = slice(p * PAIR, (p + 1) * PAIR)
        kp, vp = key_ref[:, at], value_ref[:, at]
        state = dot_tn(kp, vp)
        moved = dot_tn(kd_ref[:, at], vp) + dot_tn(kp, vd_ref[:, at])
        to = slice((p % 2) * PAIR, (p % 2 + 1) * PAIR)
        state_ref[p // 2, 0, 0, :, to] = packed_of(state).astype(BF16)
        state_ref[p // 2, 1, 0, :, to] = packed_of(moved).astype(BF16)


def flow_body(
    q_ref, s_ref, e_ref, init_ref, po_ref,
    flow_ref, qbar_ref, pbar_ref, psum_ref, prefix_ref, carry,
):
    heads = init_ref.shape[0]

    @pl.when((pl.program_id(0) == 0) & (pl.program_id(1) == 0))
    def _():
        carry[...] = e_ref[...]
        for h in range(heads):
            carry[:, h * HEAD : (h + 1) * HEAD] += init_ref[h]
        psum_ref[...] = jnp.zeros_like(psum_ref)

    carry[...] += s_ref[0, 0, 0].astype(F32)
    prefix_ref[0, 0] = carry[...].astype(BF16)
    ones = jnp.where(same_head(), 1.0, 0.0).astype(BF16)
    for p in range(heads // 2):
        at = slice(p * PAIR, (p + 1) * PAIR)
        query = q_ref[0, 0, :, at]
        prefix = spread(carry[:, at])
        mixed = dot(query, prefix)
        scale = lax.rsqrt(dot((mixed * mixed).astype(BF16), ones) * (1.0 / HEAD) + 1e-6)
        unit = mixed * scale
        flow_ref[0, 0, :, at] = unit.astype(BF16)
        cotangent = po_ref[0, 0, :, at].astype(F32)
        across = dot((unit * cotangent).astype(BF16), ones) * (1.0 / HEAD)
        mixed_bar = ((cotangent - unit * across) * scale).astype(BF16)
        pbar = packed_of(dot_tn(query, mixed_bar))
        pbar_ref[0, 0, :, at] = pbar
        psum_ref[:, at] += pbar
        qbar_ref[0, 0, :, at] = dot_nt(mixed_bar, prefix).astype(BF16)


def tangent_body(q_ref, qd_ref, prefix_ref, s_ref, e_ref, out_ref, carry):
    @pl.when((pl.program_id(0) == 0) & (pl.program_id(1) == 0))
    def _():
        carry[...] = e_ref[...]

    carry[...] += s_ref[0, 0, 0].astype(F32)
    ones = jnp.where(same_head(), 1.0, 0.0).astype(BF16)
    for p in range(carry.shape[1] // PAIR):
        at = slice(p * PAIR, (p + 1) * PAIR)
        query = q_ref[0, 0, :, at]
        prefix = spread(prefix_ref[0, 0, :, at].astype(F32))
        mixed = dot(query, prefix)
        moved = dot(qd_ref[0, 0, :, at], prefix) + dot(query, spread(carry[:, at]))
        scale = lax.rsqrt(dot((mixed * mixed).astype(BF16), ones) * (1.0 / HEAD) + 1e-6)
        unit, moved = mixed * scale, moved * scale
        along = dot((unit * moved).astype(BF16), ones) * (1.0 / HEAD)
        out_ref[0, 0, :, at] = (moved - unit * along).astype(BF16)


def suffix_body(pbar_ref, after_ref, out_ref, back_ref):
    frames, tiles = pbar_ref.shape[:2]
    heads = out_ref.shape[1]
    carry = after_ref[...]
    for f in reversed(range(frames)):
        for s in reversed(range(tiles)):
            carry = carry + pbar_ref[f, s]
            back_ref[s, f] = carry.astype(BF16)
            for h in range(heads):
                out_ref[f * tiles + s, h] = carry[:, h * HEAD : (h + 1) * HEAD]


def adjoint_body(
    key_ref, value_ref, state_ref, qbar_ref, q_ref, k_ref, v_ref, out_ref, qs, ks, vs
):
    groups, share = qbar_ref.shape[0], qbar_ref.shape[3]
    for g in range(groups):
        qs[:, g * share : (g + 1) * share] = qbar_ref[g, 0]
    for p in range(HEADS // 2):
        at = slice(p * PAIR, (p + 1) * PAIR)
        half = slice((p % 2) * PAIR, (p % 2 + 1) * PAIR)
        state = spread(state_ref[p // 2, 0, :, half].astype(F32))
        ks[:, at] = dot_nt(value_ref[:, at], state).astype(BF16)
        vs[:, at] = dot(key_ref[:, at], state).astype(BF16)
    out = dot_nt(qs[...], q_ref[...])
    out = out + dot_nt(ks[...], k_ref[...])
    out = out + dot_nt(vs[...], v_ref[...])
    out_ref[...] = out.astype(BF16)


def radices(size):
    steps, left = [], size
    if size.bit_length() % 2 == 0 and size % 2 == 0:
        steps.append(2)
        left //= 2
    while left > 1:
        step = 4 if left % 4 == 0 else left
        steps.append(step)
        left //= step
    return steps


def scan_over(total, axis, forward):
    size, place = lax.axis_size(axis), lax.axis_index(axis)
    before = jnp.zeros(total.shape, F32)
    block = 1
    steps = radices(size)
    for n, step in enumerate(steps):
        last = n == len(steps) - 1
        at = (place // block) % step
        sent = total.astype(BF16)
        for k in range(1, step):
            pairs = []
            for i in range(size):
                pos = (i // block) % step
                if forward:
                    to = pos + k
                else:
                    to = pos - k
                if last and not 0 <= to < step:
                    continue
                pairs.append((i, i + (to % step - pos) * block))
            got = lax.ppermute(sent, axis, pairs).astype(F32)
            if last:
                before = before + got
            else:
                counts = at >= k if forward else at + k < step
                before = before + jnp.where(counts, got, 0.0)
                total = total + got
        block *= step
    return before


def on_device(
    video, conv_weight, embed_weight, q_weight, k_weight, v_weight, initial_state, probe_in, probe_out
):
    groups, tms = lax.axis_size("space"), lax.axis_size("tm")
    frames, tile_rows, columns, channels = video.shape
    assert tile_rows * columns == SPAN
    tokens = frames * SPAN
    share = D // groups
    heads = HEADS // groups

    first, last = video[:, :1], video[:, -1:]
    up = [(i, i + 1) for i in range(groups - 1)]
    down = [(j, i) for i, j in up]
    both = ("tm", "space")
    prev = lax.ppermute(video, "tm", [(t, t + 1) for t in range(tms - 1)])
    above = lax.ppermute(last, "space", up)
    below = lax.ppermute(first, "space", down)
    prev_above = lax.ppermute(
        last, both, [(t * groups + i, (t + 1) * groups + j) for t in range(tms - 1) for i, j in up]
    )
    prev_below = lax.ppermute(
        first, both, [(t * groups + i, (t + 1) * groups + j) for t in range(tms - 1) for i, j in down]
    )

    weight_bytes = 2 * D * D
    row_spec = pl.BlockSpec((SPAN, D), lambda f: (f, 0))
    group_spec = pl.BlockSpec((groups, SPAN, share), lambda f: (0, f, 0))
    grouped = (group_spec, struct((groups, tokens, share), BF16))
    rowed = (row_spec, struct((tokens, D), BF16))
    w_specs = [whole(q_weight, 1)] * 3

    query_dot, key_dot, value_dot = call(
        functools.partial(probe_body, groups, share), "probe", (frames,),
        [row_spec] + w_specs, [grouped, rowed, rowed],
        (probe_in.reshape(tokens, D), q_weight, k_weight, v_weight),
        flops=6 * tokens * D * D, moved=3 * weight_bytes + 10 * tokens * D,
    )
    query_dot = lax.all_to_all(query_dot, "space", 0, 0, tiled=True)

    taps = conv_weight.reshape(3, 3, 3 * channels, -1)
    parts = (video, above, below, prev, prev_above, prev_below)
    latent = call(
        conv_body, "encode", (9,),
        [whole(a, 1) for a in parts]
        + [pl.BlockSpec((1, 1) + taps.shape[2:], lambda t: (t // 3, t % 3, 0, 0)), whole(embed_weight, 1)],
        [(pl.BlockSpec((tokens, D), lambda t: (0, 0)), struct((tokens, D), BF16))],
        parts + (taps, embed_weight),
        scratch=[
            pltpu.VMEM((2 * frames, (tile_rows + 2) * columns, 3 * channels), BF16),
            pltpu.VMEM((tokens, taps.shape[3]), F32),
        ],
        flops=2 * tokens * channels * (27 * channels + D), moved=2 * taps.size + 10 * video.size,
    )[0]

    key, value, states = call(
        state_body, "states", (frames,),
        [row_spec] + w_specs[:2] + [row_spec, row_spec],
        [
            rowed,
            rowed,
            (
                pl.BlockSpec((groups, 2, 1, HEAD, share), lambda f: (0, 0, f, 0, 0)),
                struct((groups, 2, frames, HEAD, share), BF16),
            ),
        ],
        (latent, k_weight, v_weight, key_dot, value_dot),
        flops=4 * tokens * D * D, moved=2 * weight_bytes + 10 * tokens * D,
    )
    states = lax.all_to_all(states, "space", 0, 0, tiled=True)

    query = call(
        functools.partial(query_body, groups, share), "query", (frames,),
        [row_spec, w_specs[0]], [grouped], (latent, q_weight),
        flops=2 * tokens * D * D, moved=weight_bytes + 4 * tokens * D,
    )[0]
    query = lax.all_to_all(query, "space", 0, 0, tiled=True)

    before = scan_over(states.astype(F32).sum((0, 2)), "tm", True)

    shape_sf = (groups, frames, SPAN, share)
    shape_fs = (frames, groups, SPAN, share)
    query, query_dot = query.reshape(shape_sf), query_dot.reshape(shape_sf)
    by_sf = pl.BlockSpec((1, 1, SPAN, share), lambda f, s: (s, f, 0, 0))
    by_fs = pl.BlockSpec((1, 1, SPAN, share), lambda f, s: (f, s, 0, 0))
    state_fs = pl.BlockSpec((1, 1, HEAD, share), lambda f, s: (f, s, 0, 0))
    state_shape = (frames, groups, HEAD, share)
    carried = pl.BlockSpec((HEAD, share), lambda f, s: (0, 0))

    def kind(n):
        return pl.BlockSpec((1, 1, 1, HEAD, share), lambda f, s: (s, n, f, 0, 0))

    flow, query_bar, prefix_bar, bar_sum, prefix = call(
        flow_body, "flow", (frames, groups),
        [by_sf, kind(0), carried, whole(initial_state, 2), by_fs],
        [
            (by_fs, struct(shape_fs, BF16)),
            (by_sf, struct(shape_sf, BF16)),
            (state_fs, struct(state_shape, F32)),
            (carried, struct((HEAD, share), F32)),
            (state_fs, struct(state_shape, BF16)),
        ],
        (query, states, before[0], initial_state, probe_out.reshape(shape_fs)),
        scratch=[pltpu.VMEM((HEAD, share), F32)],
        flops=20 * tokens * D * PAIR, moved=10 * tokens * D,
    )
    query_bar = lax.all_to_all(query_bar, "space", 0, 0, tiled=True)
    after = scan_over(bar_sum, "tm", False)

    tangent = call(
        tangent_body, "tangent", (frames, groups),
        [by_sf, by_sf, state_fs, kind(1), carried],
        [(by_fs, struct(shape_fs, BF16))],
        (query, query_dot, prefix, states, before[1]),
        scratch=[pltpu.VMEM((HEAD, share), F32)],
        flops=20 * tokens * D * PAIR, moved=6 * tokens * D,
    )[0]

    state_bar, state_back = call(
        suffix_body, "suffix", (),
        [pl.BlockSpec(memory_space=pltpu.VMEM)] * 2,
        [
            (pl.BlockSpec(memory_space=pltpu.VMEM), struct((frames * groups, heads, HEAD, HEAD), F32)),
            (pl.BlockSpec(memory_space=pltpu.VMEM), struct((groups, frames, HEAD, share), BF16)),
        ],
        (prefix_bar, after),
        moved=10 * frames * groups * HEAD * share,
    )
    state_back = lax.all_to_all(state_back, "space", 0, 0, tiled=True)

    adjoint = call(
        adjoint_body, "adjoint", (frames,),
        [
            row_spec,
            row_spec,
            pl.BlockSpec((groups, 1, HEAD, share), lambda f: (0, f, 0, 0)),
            pl.BlockSpec((groups, 1, SPAN, share), lambda f: (0, f, 0, 0)),
        ]
        + w_specs,
        [rowed],
        (key, value, state_back, query_bar, q_weight, k_weight, v_weight),
        scratch=[pltpu.VMEM((SPAN, D), BF16)] * 3,
        flops=6 * tokens * D * D, moved=3 * weight_bytes + 8 * tokens * D,
    )[0]
    out_shape = (frames, groups * tile_rows, columns, share)
    return (
        flow.reshape(out_shape),
        tangent.reshape(out_shape),
        adjoint.reshape(frames, tile_rows, columns, D),
        state_bar,
    )


def solution(mesh):
    in_specs = (
        P("tm", "space", None, None),
        P(),
        P(),
        P(),
        P(),
        P(),
        P("space", None, None),
        P("tm", "space", None, None),
        P("tm", None, None, "space"),
    )
    out_specs = (
        P("tm", None, None, "space"),
        P("tm", None, None, "space"),
        P("tm", "space", None, None),
        P("tm", "space", None, None),
    )
    return jax.shard_map(
        on_device, mesh=mesh, in_specs=in_specs, out_specs=out_specs, check_vma=False
    )
```

```python
import functools

import jax
import jax.numpy as jnp
from jax import lax
from jax.experimental import pallas as pl
from jax.experimental.pallas import tpu as pltpu
from jax.sharding import PartitionSpec as P

D = 1152
HEADS = 16
SPAN = 256
HEAD = D // HEADS
PAIR = 2 * HEAD
F32 = jnp.float32
BF16 = jnp.bfloat16
VMEM_BYTES = 14 * 1024 * 1024


def call(body, name, outs, args, scratch=(), flops=0, moved=0):
    vmem = pl.BlockSpec(memory_space=pltpu.VMEM)
    return pl.pallas_call(
        body,
        name=name,
        in_specs=[vmem] * len(args),
        out_specs=[vmem] * len(outs),
        out_shape=outs,
        scratch_shapes=list(scratch),
        compiler_params=pltpu.CompilerParams(vmem_limit_bytes=VMEM_BYTES),
        cost_estimate=pl.CostEstimate(flops=flops, bytes_accessed=moved, transcendentals=0),
    )(*args)


def struct(shape, dtype):
    return jax.ShapeDtypeStruct(shape, dtype)


def dot(a, b):
    return jnp.dot(a, b, preferred_element_type=F32)


def dot_nt(a, b):
    return lax.dot_general(a, b, (((1,), (1,)), ((), ())), preferred_element_type=F32)


def dot_tn(a, b):
    return lax.dot_general(a, b, (((0,), (0,)), ((), ())), preferred_element_type=F32)


def same_head():
    row = lax.broadcasted_iota(jnp.int32, (PAIR, PAIR), 0) < HEAD
    col = lax.broadcasted_iota(jnp.int32, (PAIR, PAIR), 1) < HEAD
    return row == col


def spread(packed):
    both = jnp.concatenate([packed, packed], 0)
    return jnp.where(same_head(), both, 0.0).astype(BF16)


def packed_of(square):
    col = lax.broadcasted_iota(jnp.int32, (HEAD, PAIR), 1) < HEAD
    return jnp.where(col, square[:HEAD], square[HEAD:])


def project(x, w):
    return dot(x, w).T.astype(BF16)


def mine():
    return lax.axis_index("space")


def hand_out(held, outs):
    for k, out_ref in enumerate(outs):
        out_ref[...] = held[mine() ^ k]


def take_in(parts, held):
    for k, part_ref in enumerate(parts):
        held[mine() ^ k] = part_ref[...]


def exchange(parts):
    size = lax.axis_size("space")
    return [parts[0]] + [
        lax.ppermute(parts[k], "space", [(i, i ^ k) for i in range(size)]) for k in range(1, size)
    ]


def project_groups(x, w_ref, held):
    held[...] = project(x, w_ref[...]).reshape(held.shape)


def probe_body(x_ref, w_ref, *rest):
    *outs, x_out, held = rest
    x_out[...] = x_ref[...].astype(F32).astype(BF16)
    project_groups(x_out[...], w_ref, held)
    hand_out(held, outs)


def query_body(x_ref, w_ref, *rest):
    *outs, held = rest
    project_groups(x_ref[...], w_ref, held)
    hand_out(held, outs)


def probe_pair_body(x_ref, k_ref, v_ref, out_ref):
    out_ref[0] = project(x_ref[...], k_ref[...])
    out_ref[1] = project(x_ref[...], v_ref[...])


def flip_body(po_ref, tie_ref, out_ref):
    frames, tiles = po_ref.shape[:2]

    def flip(i, _):
        f, s = i // tiles, i % tiles
        out_ref[f, s] = po_ref[f, s].astype(F32).T.astype(BF16)
        return 0

    lax.fori_loop(0, frames * tiles, flip, 0)


def conv_body(outer, own_ref, up_ref, down_ref, w_ref, out_ref, wide):
    main, source, target = outer
    frames, tile_rows, columns, channels = own_ref.shape
    tokens = tile_rows * columns
    span = (tile_rows + 2) * columns
    column = lax.broadcasted_iota(jnp.int32, (span, channels), 0) % columns
    for f in range(frames):
        mid, top, bottom = (r[f].reshape(-1, channels) for r in (own_ref, up_ref, down_ref))
        x = jnp.concatenate([top, mid, bottom], 0).astype(F32)
        left = jnp.where(column == 0, 0.0, pltpu.roll(x, 1, 0))
        right = jnp.where(column == columns - 1, 0.0, pltpu.roll(x, span - 1, 0))
        for n, part in enumerate((left, x, right)):
            part = part.astype(BF16)
            for b in range(3):
                at = (3 * b + n) * channels
                wide[f * tokens : (f + 1) * tokens, at : at + channels] = part[
                    b * columns : b * columns + tokens
                ]
    total = dot(wide[...], w_ref[main])
    extra = dot(wide[source * tokens : (source + 1) * tokens, :], w_ref[1])
    for f in range(frames):
        part = total[f * tokens : (f + 1) * tokens]
        part = part + extra if f == target else part
        out_ref[f * tokens : (f + 1) * tokens, :] = part.astype(out_ref.dtype)


def state_body(near_ref, far_ref, embed_ref, dots, k_ref, v_ref, latent, both, *rest):
    *outs, state_ref = rest
    u = near_ref[...] + far_ref[...].astype(F32)
    active = (u / (1.0 + jnp.exp(-u))).astype(BF16)
    latent[...] = dot(active, embed_ref[...]).astype(BF16)
    both[0] = project(latent[...], k_ref[...])
    both[1] = project(latent[...], v_ref[...])
    share = state_ref.shape[2] // 4

    def group(g, _):
        for half in range(share // PAIR):
            rows = pl.ds(pl.multiple_of(g * share + half * PAIR, 16), PAIR)
            for f in range(2):
                at = slice(f * SPAN, (f + 1) * SPAN)
                kt, vt = both[0, rows, at], both[1, rows, at]
                state = dot_nt(vt, kt)
                moved = dot_nt(vt, dots[0, rows, at]) + dot_nt(dots[1, rows, at], kt)
                for kind, square in enumerate((state, moved)):
                    to = (2 * f + kind) * share + half * PAIR
                    state_ref[g, :, to : to + PAIR] = packed_of(square).astype(BF16)
        return 0

    lax.fori_loop(0, state_ref.shape[0], group, 0)
    hand_out(state_ref, outs)


def total_body(*refs):
    *parts, out_ref, sent_ref = refs
    total = sum(part[...].astype(F32) for part in parts)
    width = out_ref.shape[1]
    total = total[:, :width] + total[:, width:]
    out_ref[...] = total
    sent_ref[...] = total.astype(BF16)


def before_of(gots, forward):
    counts = lax.axis_index("tm") % 2 == (1 if forward else 0)
    first = jnp.where(counts, gots[0][...].astype(F32), 0.0)
    return first + sum(got[...].astype(F32) for got in gots[1:])


def flow_body(groups, count, *refs):
    q_parts, refs = refs[:groups], refs[groups:]
    s_parts, refs = refs[:groups], refs[groups:]
    gots, refs = refs[:count], refs[count:]
    init_ref, po_ref, *refs = refs
    qbar_outs, refs = refs[:groups], refs[groups:]
    q_ref, unit_ref, scale_ref, suffix_ref, sent_ref, prefix_ref, held, s_ref, carry, qbar_ref = refs
    share = q_ref.shape[1]
    frames = prefix_ref.shape[0]
    take_in(q_parts, q_ref)
    take_in(s_parts, s_ref)
    for h in range(init_ref.shape[0]):
        held[:, h * HEAD : (h + 1) * HEAD] = init_ref[h]
    before = before_of(gots, True)[:, :share]
    for p in range(share // PAIR):
        at = slice(p * PAIR, (p + 1) * PAIR)
        packed = held[:, at]
        square = jnp.where(same_head(), jnp.concatenate([packed, packed], 0), 0.0)
        held[:, at] = packed_of(square.T) + before[:, at]
    prefix = held[...]
    for g in range(frames):
        for s in range(groups):
            prefix = prefix + s_ref[s, :, 2 * g * share : (2 * g + 1) * share].astype(F32)
            prefix_ref[g, s] = prefix.astype(BF16)
    carry[...] = jnp.zeros_like(carry)

    def frame(n, _):
        f = frames - 1 - n
        tokens = pl.ds(pl.multiple_of(f * SPAN, SPAN), SPAN)
        for s in reversed(range(groups)):
            for p in range(share // PAIR):
                at = slice(p * PAIR, (p + 1) * PAIR)
                query = q_ref[s, at, tokens]
                prefix = spread(prefix_ref[f, s, :, at].astype(F32))
                mixed = dot(prefix, query)
                bars = []
                for h in range(2):
                    rows = slice(p * PAIR + h * HEAD, p * PAIR + (h + 1) * HEAD)
                    part = mixed[h * HEAD : (h + 1) * HEAD]
                    scale = lax.rsqrt(jnp.sum(part * part, 0, keepdims=True) * (1.0 / HEAD) + 1e-6)
                    unit = part * scale
                    cotangent = po_ref[f, s, rows, :].astype(F32)
                    across = jnp.sum(unit * cotangent, 0, keepdims=True) * (1.0 / HEAD)
                    bars.append((cotangent - unit * across) * scale)
                    unit_ref[f, s, rows, :] = unit.astype(BF16)
                    scale_ref[f, s, 2 * p + h : 2 * p + h + 1, :] = scale
                mixed_bar = jnp.concatenate(bars, 0).astype(BF16)
                carry[:, at] += packed_of(dot_nt(query, mixed_bar))
                suffix_ref[s, f, :, at] = carry[:, at]
                qbar_ref[s, at, tokens] = dot_tn(prefix, mixed_bar).astype(BF16)
        return 0

    lax.fori_loop(0, frames, frame, 0)
    sent_ref[...] = carry[...].astype(BF16)
    hand_out(qbar_ref, qbar_outs)


def tangent_body(groups, count, *refs):
    qd_parts, refs = refs[:groups], refs[groups:]
    s_parts, refs = refs[:groups], refs[groups:]
    gots, refs = refs[:count], refs[count:]
    q_ref, prefix_ref, unit_ref, scale_ref, flow_ref, out_ref, qd_ref, s_ref, dots = refs
    share = q_ref.shape[1]
    frames = prefix_ref.shape[0]
    take_in(qd_parts, qd_ref)
    take_in(s_parts, s_ref)
    prefix = before_of(gots, True)[:, share:]
    for g in range(frames):
        for s in range(groups):
            prefix = prefix + s_ref[s, :, (2 * g + 1) * share : (2 * g + 2) * share].astype(F32)
            dots[g, s] = prefix.astype(BF16)

    def frame(f, _):
        tokens = pl.ds(pl.multiple_of(f * SPAN, SPAN), SPAN)
        for s in range(groups):
            outs = []
            for p in range(share // PAIR):
                at = slice(p * PAIR, (p + 1) * PAIR)
                moved = dot(spread(prefix_ref[f, s, :, at].astype(F32)), qd_ref[s, at, tokens])
                moved = moved + dot(spread(dots[f, s, :, at].astype(F32)), q_ref[s, at, tokens])
                for h in range(2):
                    rows = slice(p * PAIR + h * HEAD, p * PAIR + (h + 1) * HEAD)
                    part = moved[h * HEAD : (h + 1) * HEAD]
                    part = part * scale_ref[f, s, 2 * p + h : 2 * p + h + 1, :]
                    unit = unit_ref[f, s, rows, :].astype(F32)
                    along = jnp.sum(unit * part, 0, keepdims=True) * (1.0 / HEAD)
                    outs.append(part - unit * along)
            out_ref[f, s] = jnp.concatenate(outs, 0).T.astype(BF16)
            flow_ref[f, s] = unit_ref[f, s].astype(F32).T.astype(BF16)
        return 0

    lax.fori_loop(0, frames, frame, 0)


def back_body(count, suffix_ref, *refs):
    gots, refs = refs[:count], refs[count:]
    *outs, after_ref = refs
    after = before_of(gots, False)
    after_ref[...] = after
    for k, out_ref in enumerate(outs):
        out_ref[...] = (suffix_ref[mine() ^ k] + after).astype(BF16)


def cotangent_body(suffix_ref, after_ref, out_ref):
    tiles, frames = suffix_ref.shape[:2]
    for f in range(frames):
        for s in range(tiles):
            for h in range(out_ref.shape[1]):
                at = slice(h * HEAD, (h + 1) * HEAD)
                out_ref[f * tiles + s, h] = suffix_ref[s, f, :, at] + after_ref[:, at]


def adjoint_query_body(w_ref, *refs):
    *parts, out_ref, held = refs
    take_in(parts, held)
    out_ref[...] = dot(w_ref[...], held[...].reshape(-1, held.shape[2]))


def adjoint_body(groups, *refs):
    s_parts, refs = refs[:groups], refs[groups:]
    both, part_ref, k_ref, v_ref, out_ref, bars, state_ref = refs
    take_in(s_parts, state_ref)
    _, frames, _, share = state_ref.shape

    def group(g, _):
        for half in range(share // PAIR):
            rows = pl.ds(pl.multiple_of(g * share + half * PAIR, 16), PAIR)
            for f in range(frames):
                at = slice(f * SPAN, (f + 1) * SPAN)
                state = spread(state_ref[g, f, :, half * PAIR : (half + 1) * PAIR].astype(F32))
                bars[0, rows, at] = dot(state, both[1, rows, at]).astype(BF16)
                bars[1, rows, at] = dot_tn(state, both[0, rows, at]).astype(BF16)
        return 0

    lax.fori_loop(0, groups, group, 0)
    out = part_ref[...] + dot(k_ref[...], bars[0]) + dot(v_ref[...], bars[1])
    out_ref[...] = out.T.astype(BF16)


def scan_over(total, sent, axis, forward):
    size = lax.axis_size(axis)
    assert size % 2 == 0
    gots = [lax.ppermute(sent, axis, [(i, i ^ 1) for i in range(size)])]
    total = total + gots[0].astype(F32)
    by = 2
    while by < size:
        pairs = [(i, i + by) for i in range(size - by)]
        if not forward:
            pairs = [(j, i) for i, j in pairs]
        gots.append(lax.ppermute(total.astype(BF16), axis, pairs))
        total = total + gots[-1].astype(F32)
        by *= 2
    return gots


def on_device(
    video, conv_weight, embed_weight, q_weight, k_weight, v_weight, initial_state, probe_in, probe_out
):
    groups, tms = lax.axis_size("space"), lax.axis_size("tm")
    frames, tile_rows, columns, channels = video.shape
    assert tile_rows * columns == SPAN
    tokens = frames * SPAN
    share = D // groups
    heads = HEADS // groups

    first, last = video[:, :1], video[:, -1:]
    up = [(i, i + 1) for i in range(groups - 1)]
    down = [(j, i) for i, j in up]
    above = lax.ppermute(last, "space", up)
    below = lax.ppermute(first, "space", down)

    taps = conv_weight.reshape(3, 9 * channels, -1)
    weight_bytes = 2 * D * D

    def conv(name, outer, dtype):
        return call(
            functools.partial(conv_body, outer), name,
            [struct((tokens, taps.shape[2]), dtype)], (video, above, below, taps),
            scratch=[pltpu.VMEM((tokens, taps.shape[1]), BF16)],
            flops=27 * tokens * channels * channels, moved=taps.size + 6 * video.size,
        )[0]

    two_tall = (2, D, tokens)
    part = struct((share, tokens), BF16)
    grouped = (groups, share, tokens)
    held = pltpu.VMEM(grouped, BF16)

    *query_dot, direction = call(
        probe_body, "probe", [part] * groups + [struct((tokens, D), BF16)],
        (probe_in.reshape(tokens, D), q_weight), scratch=[held],
        flops=2 * tokens * D * D, moved=weight_bytes + 8 * tokens * D,
    )
    query_dot = exchange(query_dot)

    far = conv("conv_far", (0, 1, 0), BF16)
    far = lax.ppermute(far, "tm", [(t, t + 1) for t in range(tms - 1)])
    near = conv("conv_near", (2, 0, 1), F32)

    dots = call(
        probe_pair_body, "probe_pair", [struct(two_tall, BF16)], (direction, k_weight, v_weight),
        flops=4 * tokens * D * D, moved=2 * weight_bytes + 6 * tokens * D,
    )[0]

    state_part = struct((HEAD, 4 * share), BF16)
    latent, both, *states = call(
        state_body, "states",
        [struct((tokens, D), BF16), struct(two_tall, BF16)] + [state_part] * groups,
        (near, far, embed_weight, dots, k_weight, v_weight),
        scratch=[pltpu.VMEM((groups,) + state_part.shape, BF16)],
        flops=4 * tokens * D * D, moved=2 * weight_bytes + 14 * tokens * D,
    )
    states = exchange(states)

    query = call(
        query_body, "query", [part] * groups, (latent, q_weight), scratch=[held],
        flops=2 * tokens * D * D, moved=weight_bytes + 4 * tokens * D,
    )
    total, sent = call(
        total_body, "total",
        [struct((HEAD, 2 * share), F32), struct((HEAD, 2 * share), BF16)], states,
        moved=8 * HEAD * share * groups,
    )
    sent, query = lax.optimization_barrier((sent, query))
    query = exchange(query)
    gots = scan_over(total, sent, "tm", True)

    shape_fs = (frames, groups, SPAN, share)
    flip_fs = (frames, groups, share, SPAN)
    cotangent = call(
        flip_body, "flip", [struct(flip_fs, BF16)], (probe_out.reshape(shape_fs), sent),
        moved=6 * tokens * D,
    )[0]

    prefix_shape = (frames, groups, HEAD, share)
    state_held = pltpu.VMEM((groups,) + state_part.shape, BF16)
    *query_bar, query, unit, scale, suffix, bar_sent, prefix = call(
        functools.partial(flow_body, groups, len(gots)), "flow",
        [part] * groups
        + [
            struct(grouped, BF16),
            struct(flip_fs, BF16),
            struct((frames, groups, heads, SPAN), F32),
            struct((groups, frames, HEAD, share), F32),
            struct((HEAD, share), BF16),
            struct(prefix_shape, BF16),
        ],
        (*query, *states, *gots, initial_state, cotangent),
        scratch=[pltpu.VMEM((HEAD, share), F32), state_held, pltpu.VMEM((HEAD, share), F32), held],
        flops=12 * tokens * D * PAIR, moved=10 * tokens * D,
    )
    query_bar = exchange(query_bar)
    bar_gots = scan_over(suffix[0, 0], bar_sent, "tm", False)

    flow, tangent = call(
        functools.partial(tangent_body, groups, len(gots)), "tangent", [struct(shape_fs, BF16)] * 2,
        (*query_dot, *states, *gots, query, prefix, unit, scale),
        scratch=[held, state_held, pltpu.VMEM(prefix_shape, BF16)],
        flops=12 * tokens * D * PAIR, moved=10 * tokens * D,
    )

    *state_back, after = call(
        functools.partial(back_body, len(bar_gots)), "back",
        [struct((frames, HEAD, share), BF16)] * groups + [struct((HEAD, share), F32)],
        (suffix, *bar_gots), moved=10 * frames * groups * HEAD * share,
    )
    state_back, flow, tangent = lax.optimization_barrier((state_back, flow, tangent))
    state_back = exchange(state_back)
    state_bar = call(
        cotangent_body, "cotangent", [struct((frames * groups, heads, HEAD, HEAD), F32)],
        (suffix, after), moved=10 * frames * groups * HEAD * share,
    )[0]
    query_part = call(
        adjoint_query_body, "adjoint_query", [struct((D, tokens), F32)], (q_weight, *query_bar),
        scratch=[held], flops=2 * tokens * D * D, moved=weight_bytes + 6 * tokens * D,
    )[0]
    adjoint = call(
        functools.partial(adjoint_body, groups), "adjoint", [struct((tokens, D), BF16)],
        (*state_back, both, query_part, k_weight, v_weight),
        scratch=[pltpu.VMEM(two_tall, BF16), pltpu.VMEM((groups, frames, HEAD, share), BF16)],
        flops=4 * tokens * D * D, moved=2 * weight_bytes + 10 * tokens * D,
    )[0]
    out_shape = (frames, groups * tile_rows, columns, share)
    return (
        flow.reshape(out_shape),
        tangent.reshape(out_shape),
        adjoint.reshape(frames, tile_rows, columns, D),
        state_bar,
    )


def solution(mesh):
    in_specs = (
        P("tm", "space", None, None),
        P(),
        P(),
        P(),
        P(),
        P(),
        P("space", None, None),
        P("tm", "space", None, None),
        P("tm", None, None, "space"),
    )
    out_specs = (
        P("tm", None, None, "space"),
        P("tm", None, None, "space"),
        P("tm", "space", None, None),
        P("tm", "space", None, None),
    )
    return jax.shard_map(
        on_device, mesh=mesh, in_specs=in_specs, out_specs=out_specs, check_vma=False
    )
```

```python
import functools

import jax
import jax.numpy as jnp
from jax import lax
from jax.experimental import pallas as pl
from jax.experimental.pallas import tpu as pltpu
from jax.sharding import PartitionSpec as P


D = 1152
HEADS = 16
SPAN = 256
HEAD = D // HEADS
PAIR = 2 * HEAD
F32 = jnp.float32
BF16 = jnp.bfloat16
VMEM_BYTES = 14 * 1024 * 1024


def call(body, outs, args, scratch=(), flops=0, moved=0, far=0):
    vmem = pl.BlockSpec(memory_space=pltpu.VMEM)
    anywhere = pl.BlockSpec(memory_space=pltpu.HBM)
    args = [pltpu.with_memory_space_constraint(a, pltpu.HBM) for a in args[:far]] + list(args[far:])
    return pl.pallas_call(
        body,
        in_specs=[anywhere] * far + [vmem] * (len(args) - far),
        out_specs=[vmem] * len(outs),
        out_shape=outs,
        scratch_shapes=list(scratch),
        compiler_params=pltpu.CompilerParams(vmem_limit_bytes=VMEM_BYTES),
        cost_estimate=pl.CostEstimate(flops=flops, bytes_accessed=moved, transcendentals=0),
    )(*args)


def struct(shape, dtype):
    return jax.ShapeDtypeStruct(shape, dtype)


def dot(a, b):
    return jnp.dot(a, b, preferred_element_type=F32)


def dot_nt(a, b):
    return lax.dot_general(a, b, (((1,), (1,)), ((), ())), preferred_element_type=F32)


def dot_tn(a, b):
    return lax.dot_general(a, b, (((0,), (0,)), ((), ())), preferred_element_type=F32)


def same_head():
    row = lax.broadcasted_iota(jnp.int32, (PAIR, PAIR), 0) < HEAD
    col = lax.broadcasted_iota(jnp.int32, (PAIR, PAIR), 1) < HEAD
    return row == col


def spread(packed):
    both = jnp.concatenate([packed, packed], 0)
    return jnp.where(same_head(), both, 0.0).astype(BF16)


def packed_of(square):
    col = lax.broadcasted_iota(jnp.int32, (HEAD, PAIR), 1) < HEAD
    return jnp.where(col, square[:HEAD], square[HEAD:])


def project(x, w):
    return dot(x, w).T.astype(BF16)


def mine():
    return lax.axis_index("space")


def hand_out(held, outs):
    for k, out_ref in enumerate(outs):
        out_ref[...] = held[mine() ^ k]


def take_in(parts, held):
    for k, part_ref in enumerate(parts):
        held[mine() ^ k] = part_ref[...]


def exchange(parts):
    size = lax.axis_size("space")
    got = [parts[0]]
    for k in range(1, size):
        got.append(lax.ppermute(parts[k], "space", [(i, i ^ k) for i in range(size)]))
    return got


def project_groups(x, w_ref, held):
    held[...] = project(x, w_ref[...]).reshape(held.shape)


def probe_body(x_hbm, w_hbm, taps_hbm, *rest):
    *outs, x_out, w_ref, taps_ref, x_ref, held, sems = rest
    copies = [
        pltpu.make_async_copy(source, target, sems.at[i])
        for i, (source, target) in enumerate(
            ((x_hbm, x_ref), (w_hbm, w_ref), (taps_hbm, taps_ref))
        )
    ]
    copies[0].start()
    copies[1].start()
    copies[0].wait()
    x_out[...] = x_ref[...].astype(F32).astype(BF16)
    copies[1].wait()
    copies[2].start()
    project_groups(x_out[...], w_ref, held)
    hand_out(held, outs)
    copies[2].wait()


def query_body(x_ref, w_ref, *rest):
    *outs, held = rest
    project_groups(x_ref[...], w_ref, held)
    hand_out(held, outs)


def probe_pair_body(x_ref, k_ref, v_ref, out_ref):
    out_ref[0] = project(x_ref[...], k_ref[...])
    out_ref[1] = project(x_ref[...], v_ref[...])


def flip_body(po_ref, tie_ref, out_ref):
    frames, tiles = po_ref.shape[:2]

    def flip(i, _):
        f, s = i // tiles, i % tiles
        out_ref[f, s] = po_ref[f, s].astype(F32).T.astype(BF16)
        return 0

    lax.fori_loop(0, frames * tiles, flip, 0)


def conv_body(outer, own_ref, up_ref, down_ref, w_ref, out_ref, wide):
    main, source, target = outer
    frames, tile_rows, columns, channels = own_ref.shape
    tokens = tile_rows * columns
    span = (tile_rows + 2) * columns
    column = lax.broadcasted_iota(jnp.int32, (span, channels), 0) % columns
    for f in range(frames):
        mid, top, bottom = (r[f].reshape(-1, channels) for r in (own_ref, up_ref, down_ref))
        x = jnp.concatenate([top, mid, bottom], 0).astype(F32)
        left = jnp.where(column == 0, 0.0, pltpu.roll(x, 1, 0))
        right = jnp.where(column == columns - 1, 0.0, pltpu.roll(x, span - 1, 0))
        for n, part in enumerate((left, x, right)):
            part = part.astype(BF16)
            for b in range(3):
                at = (3 * b + n) * channels
                wide[f * tokens : (f + 1) * tokens, at : at + channels] = part[
                    b * columns : b * columns + tokens
                ]
    total = dot(wide[...], w_ref[main])
    extra = dot(wide[source * tokens : (source + 1) * tokens, :], w_ref[1])
    for f in range(frames):
        part = total[f * tokens : (f + 1) * tokens]
        part = part + extra if f == target else part
        out_ref[f * tokens : (f + 1) * tokens, :] = part.astype(out_ref.dtype)


def state_body(near_ref, far_ref, embed_ref, dots, k_ref, v_ref, latent, both, *rest):
    *outs, state_ref = rest
    groups = state_ref.shape[1]
    u = near_ref[...] + far_ref[...].astype(F32)
    active = (u / (1.0 + jnp.exp(-u))).astype(BF16)
    latent[...] = dot(active, embed_ref[...]).astype(BF16)
    both[0] = project(latent[...], k_ref[...])
    both[1] = project(latent[...], v_ref[...])
    share = state_ref.shape[3] // 2

    def group(g, _):
        for half in range(share // PAIR):
            rows = pl.ds(pl.multiple_of(g * share + half * PAIR, 16), PAIR)
            blocks = []
            for f in range(2):
                at = slice(f * SPAN, (f + 1) * SPAN)
                kt, vt = both[0, rows, at], both[1, rows, at]
                state = dot_nt(vt, kt)
                moved = dot_nt(vt, dots[0, rows, at]) + dot_nt(dots[1, rows, at], kt)
                blocks.append((packed_of(state), packed_of(moved)))
            for kind in range(2):
                to = kind * share + half * PAIR
                first, second = blocks[0][kind], blocks[1][kind]
                state_ref[0, g, :, to : to + PAIR] = (first + second).astype(BF16)
                state_ref[1, g, :, to : to + PAIR] = first.astype(BF16)
        return 0

    lax.fori_loop(0, groups, group, 0)
    hand_out(state_ref.at[0], outs[:groups])
    hand_out(state_ref.at[1], outs[groups:])


def total_body(*refs):
    *parts, out_ref, sent_ref = refs
    total = sum(part[...].astype(F32) for part in parts)
    out_ref[...] = total
    sent_ref[...] = total.astype(BF16)


def prefixes(start, sums, firsts, at, held, out_ref):
    groups = len(sums)
    for k in range(groups):
        first = firsts[k][:, at].astype(F32)
        held[0, mine() ^ k] = first
        held[1, mine() ^ k] = sums[k][:, at].astype(F32) - first
    for f in range(2):
        for s in range(groups):
            start = start + held[f, s]
            out_ref[f, s] = start.astype(BF16)


def before_of(gots, forward):
    counts = lax.axis_index("tm") % 2 == (1 if forward else 0)
    first = jnp.where(counts, gots[0][...].astype(F32), 0.0)
    return first + sum(got[...].astype(F32) for got in gots[1:])


def flow_body(groups, count, *refs):
    q_parts, refs = refs[:groups], refs[groups:]
    sums, firsts, refs = refs[:groups], refs[groups : 2 * groups], refs[2 * groups :]
    gots, refs = refs[:count], refs[count:]
    init_ref, po_ref, *refs = refs
    qbar_outs, refs = refs[:groups], refs[groups:]
    q_ref, unit_ref, scale_ref, suffix_ref, sent_ref, prefix_ref, held, s_ref, carry, qbar_ref = refs
    share = q_ref.shape[1]
    frames = prefix_ref.shape[0]
    take_in(q_parts, q_ref)
    for h in range(init_ref.shape[0]):
        held[:, h * HEAD : (h + 1) * HEAD] = init_ref[h]
    before = before_of(gots, True)[:, :share]
    for p in range(share // PAIR):
        at = slice(p * PAIR, (p + 1) * PAIR)
        packed = held[:, at]
        square = jnp.where(same_head(), jnp.concatenate([packed, packed], 0), 0.0)
        held[:, at] = packed_of(square.T) + before[:, at]
    prefixes(held[...], sums, firsts, slice(0, share), s_ref, prefix_ref)
    carry[...] = jnp.zeros_like(carry)

    def frame(n, _):
        f = frames - 1 - n
        tokens = pl.ds(pl.multiple_of(f * SPAN, SPAN), SPAN)
        for s in reversed(range(groups)):
            for p in range(share // PAIR):
                at = slice(p * PAIR, (p + 1) * PAIR)
                query = q_ref[s, at, tokens]
                prefix = spread(prefix_ref[f, s, :, at].astype(F32))
                mixed = dot(prefix, query)
                bars = []
                for h in range(2):
                    rows = slice(p * PAIR + h * HEAD, p * PAIR + (h + 1) * HEAD)
                    part = mixed[h * HEAD : (h + 1) * HEAD]
                    scale = lax.rsqrt(jnp.sum(part * part, 0, keepdims=True) * (1.0 / HEAD) + 1e-6)
                    unit = part * scale
                    cotangent = po_ref[f, s, rows, :].astype(F32)
                    across = jnp.sum(unit * cotangent, 0, keepdims=True) * (1.0 / HEAD)
                    bars.append((cotangent - unit * across) * scale)
                    unit_ref[f, s, rows, :] = unit.astype(BF16)
                    scale_ref[f, s, 2 * p + h : 2 * p + h + 1, :] = scale
                mixed_bar = jnp.concatenate(bars, 0).astype(BF16)
                carry[:, at] += packed_of(dot_nt(query, mixed_bar))
                suffix_ref[s, f, :, at] = carry[:, at]
                qbar_ref[s, at, tokens] = dot_tn(prefix, mixed_bar).astype(BF16)
        return 0

    lax.fori_loop(0, frames, frame, 0)
    sent_ref[...] = carry[...].astype(BF16)
    hand_out(qbar_ref, qbar_outs)


def tangent_body(groups, count, *refs):
    qd_parts, refs = refs[:groups], refs[groups:]
    sums, firsts, refs = refs[:groups], refs[groups : 2 * groups], refs[2 * groups :]
    gots, refs = refs[:count], refs[count:]
    q_ref, prefix_ref, unit_ref, scale_ref, flow_ref, out_ref, qd_ref, s_ref, dots = refs
    share = q_ref.shape[1]
    frames = prefix_ref.shape[0]
    take_in(qd_parts, qd_ref)
    before = before_of(gots, True)[:, share:]
    prefixes(before, sums, firsts, slice(share, 2 * share), s_ref, dots)

    def frame(f, _):
        tokens = pl.ds(pl.multiple_of(f * SPAN, SPAN), SPAN)
        for s in range(groups):
            outs = []
            for p in range(share // PAIR):
                at = slice(p * PAIR, (p + 1) * PAIR)
                moved = dot(spread(prefix_ref[f, s, :, at].astype(F32)), qd_ref[s, at, tokens])
                moved = moved + dot(spread(dots[f, s, :, at].astype(F32)), q_ref[s, at, tokens])
                for h in range(2):
                    rows = slice(p * PAIR + h * HEAD, p * PAIR + (h + 1) * HEAD)
                    part = moved[h * HEAD : (h + 1) * HEAD]
                    part = part * scale_ref[f, s, 2 * p + h : 2 * p + h + 1, :]
                    unit = unit_ref[f, s, rows, :].astype(F32)
                    along = jnp.sum(unit * part, 0, keepdims=True) * (1.0 / HEAD)
                    outs.append(part - unit * along)
            out_ref[f, s] = jnp.concatenate(outs, 0).T.astype(BF16)
            flow_ref[f, s] = unit_ref[f, s].astype(F32).T.astype(BF16)
        return 0

    lax.fori_loop(0, frames, frame, 0)


def back_body(count, suffix_ref, *refs):
    gots, refs = refs[:count], refs[count:]
    *outs, after_ref = refs
    after = before_of(gots, False)
    after_ref[...] = after
    for k, out_ref in enumerate(outs):
        out_ref[...] = (suffix_ref[mine() ^ k] + after).astype(BF16)


def cotangent_body(suffix_ref, after_ref, out_ref):
    tiles, frames = suffix_ref.shape[:2]
    for f in range(frames):
        for s in range(tiles):
            for h in range(out_ref.shape[1]):
                at = slice(h * HEAD, (h + 1) * HEAD)
                out_ref[f * tiles + s, h] = suffix_ref[s, f, :, at] + after_ref[:, at]


def adjoint_query_body(w_ref, *refs):
    *parts, out_ref, held = refs
    take_in(parts, held)
    out_ref[...] = dot(w_ref[...], held[...].reshape(-1, held.shape[2]))


def adjoint_body(groups, *refs):
    s_parts, refs = refs[:groups], refs[groups:]
    both, part_ref, k_ref, v_ref, out_ref, bars, state_ref = refs
    take_in(s_parts, state_ref)
    _, frames, _, share = state_ref.shape

    def group(g, _):
        for half in range(share // PAIR):
            rows = pl.ds(pl.multiple_of(g * share + half * PAIR, 16), PAIR)
            for f in range(frames):
                at = slice(f * SPAN, (f + 1) * SPAN)
                state = spread(state_ref[g, f, :, half * PAIR : (half + 1) * PAIR].astype(F32))
                bars[0, rows, at] = dot(state, both[1, rows, at]).astype(BF16)
                bars[1, rows, at] = dot_tn(state, both[0, rows, at]).astype(BF16)
        return 0

    lax.fori_loop(0, groups, group, 0)
    out = part_ref[...] + dot(k_ref[...], bars[0]) + dot(v_ref[...], bars[1])
    out_ref[...] = out.T.astype(BF16)


def scan_over(total, sent, axis, forward):
    size = lax.axis_size(axis)
    assert size % 2 == 0
    gots = [lax.ppermute(sent, axis, [(i, i ^ 1) for i in range(size)])]
    total = total + gots[0].astype(F32)
    by = 2
    while by < size:
        pairs = [(i, i + by) for i in range(size - by)]
        if not forward:
            pairs = [(j, i) for i, j in pairs]
        gots.append(lax.ppermute(total.astype(BF16), axis, pairs))
        total = total + gots[-1].astype(F32)
        by *= 2
    return gots


def on_device(
    video, conv_weight, embed_weight, q_weight, k_weight, v_weight, initial_state, probe_in, probe_out
):
    groups, tms = lax.axis_size("space"), lax.axis_size("tm")
    frames, tile_rows, columns, channels = video.shape
    assert tile_rows * columns == SPAN
    tokens = frames * SPAN
    share = D // groups
    heads = HEADS // groups

    first, last = video[:, :1], video[:, -1:]
    up = [(i, i + 1) for i in range(groups - 1)]
    down = [(j, i) for i, j in up]
    above = lax.ppermute(last, "space", up)
    below = lax.ppermute(first, "space", down)

    taps = conv_weight.reshape(3, 9 * channels, -1)
    weight_bytes = 2 * D * D

    def conv(outer, dtype):
        return call(
            functools.partial(conv_body, outer),
            [struct((tokens, taps.shape[2]), dtype)], (video, above, below, taps),
            scratch=[pltpu.VMEM((tokens, taps.shape[1]), BF16)],
            flops=27 * tokens * channels * channels, moved=taps.size + 6 * video.size,
        )[0]

    two_tall = (2, D, tokens)
    part = struct((share, tokens), BF16)
    grouped = (groups, share, tokens)
    held = pltpu.VMEM(grouped, BF16)

    *query_dot, direction, q_near, taps = call(
        probe_body,
        [part] * groups
        + [struct((tokens, D), BF16), struct(q_weight.shape, BF16), struct(taps.shape, BF16)],
        (probe_in.reshape(tokens, D), q_weight, taps), far=3,
        scratch=[pltpu.VMEM((tokens, D), jnp.int32), held, pltpu.SemaphoreType.DMA((3,))],
        flops=2 * tokens * D * D, moved=weight_bytes + 8 * tokens * D,
    )
    query_dot = exchange(query_dot)

    far = conv((0, 1, 0), BF16)
    far = lax.ppermute(far, "tm", [(t, t + 1) for t in range(tms - 1)])
    near = conv((2, 0, 1), F32)

    dots = call(
        probe_pair_body, [struct(two_tall, BF16)], (direction, k_weight, v_weight),
        flops=4 * tokens * D * D, moved=2 * weight_bytes + 6 * tokens * D,
    )[0]

    assert frames == 2
    state_part = struct((HEAD, 2 * share), BF16)
    latent, both, *states = call(
        state_body,
        [struct((tokens, D), BF16), struct(two_tall, BF16)] + [state_part] * (2 * groups),
        (near, far, embed_weight, dots, k_weight, v_weight),
        scratch=[pltpu.VMEM((2, groups) + state_part.shape, BF16)],
        flops=4 * tokens * D * D, moved=2 * weight_bytes + 14 * tokens * D,
    )
    sums, firsts = exchange(states[:groups]), states[groups:]

    query = call(
        query_body, [part] * groups, (latent, q_near), scratch=[held],
        flops=2 * tokens * D * D, moved=weight_bytes + 4 * tokens * D,
    )
    total, sent = call(
        total_body,
        [struct((HEAD, 2 * share), F32), struct((HEAD, 2 * share), BF16)], sums,
        moved=8 * HEAD * share * groups,
    )
    query = exchange(query)
    firsts = exchange(firsts)
    gots = scan_over(total, sent, "tm", True)

    shape_fs = (frames, groups, SPAN, share)
    flip_fs = (frames, groups, share, SPAN)
    cotangent = call(
        flip_body, [struct(flip_fs, BF16)], (probe_out.reshape(shape_fs), sent),
        moved=6 * tokens * D,
    )[0]

    prefix_shape = (frames, groups, HEAD, share)
    state_held = pltpu.VMEM(prefix_shape, F32)
    *query_bar, query, unit, scale, suffix, bar_sent, prefix = call(
        functools.partial(flow_body, groups, len(gots)),
        [part] * groups
        + [
            struct(grouped, BF16),
            struct(flip_fs, BF16),
            struct((frames, groups, heads, SPAN), F32),
            struct((groups, frames, HEAD, share), F32),
            struct((HEAD, share), BF16),
            struct(prefix_shape, BF16),
        ],
        (*query, *sums, *firsts, *gots, initial_state, cotangent),
        scratch=[pltpu.VMEM((HEAD, share), F32), state_held, pltpu.VMEM((HEAD, share), F32), held],
        flops=12 * tokens * D * PAIR, moved=10 * tokens * D,
    )
    query_bar = exchange(query_bar)
    bar_gots = scan_over(suffix[0, 0], bar_sent, "tm", False)

    flow, tangent = call(
        functools.partial(tangent_body, groups, len(gots)), [struct(shape_fs, BF16)] * 2,
        (*query_dot, *sums, *firsts, *gots, query, prefix, unit, scale),
        scratch=[held, state_held, pltpu.VMEM(prefix_shape, BF16)],
        flops=12 * tokens * D * PAIR, moved=10 * tokens * D,
    )

    *state_back, after = call(
        functools.partial(back_body, len(bar_gots)),
        [struct((frames, HEAD, share), BF16)] * groups + [struct((HEAD, share), F32)],
        (suffix, *bar_gots), moved=10 * frames * groups * HEAD * share,
    )
    state_back, flow, tangent = lax.optimization_barrier((state_back, flow, tangent))
    state_back = exchange(state_back)
    state_bar = call(
        cotangent_body, [struct((frames * groups, heads, HEAD, HEAD), F32)],
        (suffix, after), moved=10 * frames * groups * HEAD * share,
    )[0]
    query_part = call(
        adjoint_query_body, [struct((D, tokens), F32)], (q_near, *query_bar),
        scratch=[held], flops=2 * tokens * D * D, moved=weight_bytes + 6 * tokens * D,
    )[0]
    adjoint = call(
        functools.partial(adjoint_body, groups), [struct((tokens, D), BF16)],
        (*state_back, both, query_part, k_weight, v_weight),
        scratch=[pltpu.VMEM(two_tall, BF16), pltpu.VMEM((groups, frames, HEAD, share), BF16)],
        flops=4 * tokens * D * D, moved=2 * weight_bytes + 10 * tokens * D,
    )[0]
    out_shape = (frames, groups * tile_rows, columns, share)
    return (
        flow.reshape(out_shape),
        tangent.reshape(out_shape),
        adjoint.reshape(frames, tile_rows, columns, D),
        state_bar,
    )


def solution(mesh):
    in_specs = (
        P("tm", "space", None, None),
        P(),
        P(),
        P(),
        P(),
        P(),
        P("space", None, None),
        P("tm", "space", None, None),
        P("tm", None, None, "space"),
    )
    out_specs = (
        P("tm", None, None, "space"),
        P("tm", None, None, "space"),
        P("tm", "space", None, None),
        P("tm", "space", None, None),
    )
    return jax.shard_map(
        on_device, mesh=mesh, in_specs=in_specs, out_specs=out_specs, check_vma=False
    )
```

```python
import functools

import jax
import jax.numpy as jnp
from jax import lax
from jax.experimental import pallas as pl
from jax.experimental.pallas import tpu as pltpu
from jax.sharding import PartitionSpec as P


D = 1152
HEADS = 16
SPAN = 256
HEAD = D // HEADS
PAIR = 2 * HEAD
F32 = jnp.float32
BF16 = jnp.bfloat16
VMEM_BYTES = 14 * 1024 * 1024


def call(body, outs, args, scratch=(), flops=0, moved=0, far=0):
    vmem = pl.BlockSpec(memory_space=pltpu.VMEM)
    anywhere = pl.BlockSpec(memory_space=pltpu.HBM)
    args = [pltpu.with_memory_space_constraint(a, pltpu.HBM) for a in args[:far]] + list(args[far:])
    return pl.pallas_call(
        body,
        in_specs=[anywhere] * far + [vmem] * (len(args) - far),
        out_specs=[vmem] * len(outs),
        out_shape=outs,
        scratch_shapes=list(scratch),
        compiler_params=pltpu.CompilerParams(vmem_limit_bytes=VMEM_BYTES),
        cost_estimate=pl.CostEstimate(flops=flops, bytes_accessed=moved, transcendentals=0),
    )(*args)


def struct(shape, dtype):
    return jax.ShapeDtypeStruct(shape, dtype)


def dot(a, b):
    return jnp.dot(a, b, preferred_element_type=F32)


def dot_nt(a, b):
    return lax.dot_general(a, b, (((1,), (1,)), ((), ())), preferred_element_type=F32)


def dot_tn(a, b):
    return lax.dot_general(a, b, (((0,), (0,)), ((), ())), preferred_element_type=F32)


def same_head():
    row = lax.broadcasted_iota(jnp.int32, (PAIR, PAIR), 0) < HEAD
    col = lax.broadcasted_iota(jnp.int32, (PAIR, PAIR), 1) < HEAD
    return row == col


def spread(packed):
    both = jnp.concatenate([packed, packed], 0)
    return jnp.where(same_head(), both, 0.0).astype(BF16)


def packed_of(square):
    col = lax.broadcasted_iota(jnp.int32, (HEAD, PAIR), 1) < HEAD
    return jnp.where(col, square[:HEAD], square[HEAD:])


def project(x, w):
    return dot(x, w).T.astype(BF16)


def mine():
    return lax.axis_index("space")


def hand_out(held, outs):
    for k, out_ref in enumerate(outs):
        out_ref[...] = held[mine() ^ k]


def take_in(parts, held):
    for k, part_ref in enumerate(parts):
        held[mine() ^ k] = part_ref[...]


def exchange(parts):
    size = lax.axis_size("space")
    got = [parts[0]]
    for k in range(1, size):
        got.append(lax.ppermute(parts[k], "space", [(i, i ^ k) for i in range(size)]))
    return got


def project_groups(x, w_ref, held):
    held[...] = project(x, w_ref[...]).reshape(held.shape)


def probe_body(x_hbm, w_hbm, taps_hbm, *rest):
    *outs, x_out, w_ref, taps_ref, x_ref, held, sems = rest
    copies = [
        pltpu.make_async_copy(source, target, sems.at[i])
        for i, (source, target) in enumerate(
            ((x_hbm, x_ref), (w_hbm, w_ref), (taps_hbm.at[pl.ds(0, 2)], taps_ref))
        )
    ]
    copies[0].start()
    copies[1].start()
    copies[0].wait()
    x_out[...] = x_ref[...].astype(F32).astype(BF16)
    copies[1].wait()
    copies[2].start()
    project_groups(x_out[...], w_ref, held)
    hand_out(held, outs)
    copies[2].wait()


def query_body(x_ref, w_ref, *rest):
    *outs, held = rest
    project_groups(x_ref[...], w_ref, held)
    hand_out(held, outs)


def probe_pair_body(taps_hbm, x_ref, k_ref, v_ref, out_ref, taps_ref, sem):
    copy = pltpu.make_async_copy(taps_hbm.at[2], taps_ref, sem)
    copy.start()
    out_ref[0] = project(x_ref[...], k_ref[...])
    out_ref[1] = project(x_ref[...], v_ref[...])
    copy.wait()


def flip_body(po_ref, tie_ref, out_ref):
    frames, tiles = po_ref.shape[:2]

    def flip(i, _):
        f, s = i // tiles, i % tiles
        out_ref[f, s] = po_ref[f, s].astype(F32).T.astype(BF16)
        return 0

    lax.fori_loop(0, frames * tiles, flip, 0)


def conv_body(source, target, own_ref, up_ref, down_ref, main_ref, mid_ref, out_ref, wide):
    frames, tile_rows, columns, channels = own_ref.shape
    tokens = tile_rows * columns
    span = (tile_rows + 2) * columns
    column = lax.broadcasted_iota(jnp.int32, (span, channels), 0) % columns
    for f in range(frames):
        mid, top, bottom = (r[f].reshape(-1, channels) for r in (own_ref, up_ref, down_ref))
        x = jnp.concatenate([top, mid, bottom], 0).astype(F32)
        left = jnp.where(column == 0, 0.0, pltpu.roll(x, 1, 0))
        right = jnp.where(column == columns - 1, 0.0, pltpu.roll(x, span - 1, 0))
        for n, part in enumerate((left, x, right)):
            part = part.astype(BF16)
            for b in range(3):
                at = (3 * b + n) * channels
                wide[f * tokens : (f + 1) * tokens, at : at + channels] = part[
                    b * columns : b * columns + tokens
                ]
    total = dot(wide[...], main_ref[...] if len(main_ref.shape) == 2 else main_ref[0])
    extra = dot(wide[source * tokens : (source + 1) * tokens, :], mid_ref[1])
    for f in range(frames):
        part = total[f * tokens : (f + 1) * tokens]
        part = part + extra if f == target else part
        out_ref[f * tokens : (f + 1) * tokens, :] = part.astype(out_ref.dtype)


def state_body(near_ref, far_ref, embed_ref, dots, k_ref, v_ref, latent, both, *rest):
    *outs, state_ref = rest
    groups = state_ref.shape[1]
    u = near_ref[...] + far_ref[...].astype(F32)
    active = (u / (1.0 + jnp.exp(-u))).astype(BF16)
    latent[...] = dot(active, embed_ref[...]).astype(BF16)
    both[0] = project(latent[...], k_ref[...])
    both[1] = project(latent[...], v_ref[...])
    share = state_ref.shape[3] // 2

    def group(g, _):
        for half in range(share // PAIR):
            rows = pl.ds(pl.multiple_of(g * share + half * PAIR, 16), PAIR)
            blocks = []
            for f in range(2):
                at = slice(f * SPAN, (f + 1) * SPAN)
                kt, vt = both[0, rows, at], both[1, rows, at]
                state = dot_nt(vt, kt)
                moved = dot_nt(vt, dots[0, rows, at]) + dot_nt(dots[1, rows, at], kt)
                blocks.append((packed_of(state), packed_of(moved)))
            for kind in range(2):
                to = kind * share + half * PAIR
                first, second = blocks[0][kind], blocks[1][kind]
                state_ref[0, g, :, to : to + PAIR] = (first + second).astype(BF16)
                state_ref[1, g, :, to : to + PAIR] = first.astype(BF16)
        return 0

    lax.fori_loop(0, groups, group, 0)
    hand_out(state_ref.at[0], outs[:groups])
    hand_out(state_ref.at[1], outs[groups:])


def total_body(*refs):
    *parts, out_ref, sent_ref = refs
    total = sum(part[...].astype(F32) for part in parts)
    out_ref[...] = total
    sent_ref[...] = total.astype(BF16)


def prefixes(start, sums, firsts, at, held, out_ref):
    groups = len(sums)
    for k in range(groups):
        first = firsts[k][:, at].astype(F32)
        held[0, mine() ^ k] = first
        held[1, mine() ^ k] = sums[k][:, at].astype(F32) - first
    for f in range(2):
        for s in range(groups):
            start = start + held[f, s]
            out_ref[f, s] = start.astype(BF16)


def before_of(gots, forward):
    counts = lax.axis_index("tm") % 2 == (1 if forward else 0)
    first = jnp.where(counts, gots[0][...].astype(F32), 0.0)
    return first + sum(got[...].astype(F32) for got in gots[1:])


def flow_body(groups, count, *refs):
    q_parts, refs = refs[:groups], refs[groups:]
    sums, firsts, refs = refs[:groups], refs[groups : 2 * groups], refs[2 * groups :]
    gots, refs = refs[:count], refs[count:]
    init_ref, po_ref, *refs = refs
    qbar_outs, refs = refs[:groups], refs[groups:]
    q_ref, unit_ref, scale_ref, suffix_ref, sent_ref, prefix_ref, held, s_ref, carry, qbar_ref = refs
    share = q_ref.shape[1]
    frames = prefix_ref.shape[0]
    take_in(q_parts, q_ref)
    for h in range(init_ref.shape[0]):
        held[:, h * HEAD : (h + 1) * HEAD] = init_ref[h]
    before = before_of(gots, True)[:, :share]
    for p in range(share // PAIR):
        at = slice(p * PAIR, (p + 1) * PAIR)
        packed = held[:, at]
        square = jnp.where(same_head(), jnp.concatenate([packed, packed], 0), 0.0)
        held[:, at] = packed_of(square.T) + before[:, at]
    prefixes(held[...], sums, firsts, slice(0, share), s_ref, prefix_ref)
    carry[...] = jnp.zeros_like(carry)

    def frame(n, _):
        f = frames - 1 - n
        tokens = pl.ds(pl.multiple_of(f * SPAN, SPAN), SPAN)
        for s in reversed(range(groups)):
            for p in range(share // PAIR):
                at = slice(p * PAIR, (p + 1) * PAIR)
                query = q_ref[s, at, tokens]
                prefix = spread(prefix_ref[f, s, :, at].astype(F32))
                mixed = dot(prefix, query)
                bars = []
                for h in range(2):
                    rows = slice(p * PAIR + h * HEAD, p * PAIR + (h + 1) * HEAD)
                    part = mixed[h * HEAD : (h + 1) * HEAD]
                    scale = lax.rsqrt(jnp.sum(part * part, 0, keepdims=True) * (1.0 / HEAD) + 1e-6)
                    unit = part * scale
                    cotangent = po_ref[f, s, rows, :].astype(F32)
                    across = jnp.sum(unit * cotangent, 0, keepdims=True) * (1.0 / HEAD)
                    bars.append((cotangent - unit * across) * scale)
                    unit_ref[f, s, rows, :] = unit.astype(BF16)
                    scale_ref[f, s, 2 * p + h : 2 * p + h + 1, :] = scale
                mixed_bar = jnp.concatenate(bars, 0).astype(BF16)
                carry[:, at] += packed_of(dot_nt(query, mixed_bar))
                suffix_ref[s, f, :, at] = carry[:, at]
                qbar_ref[s, at, tokens] = dot_tn(prefix, mixed_bar).astype(BF16)
        return 0

    lax.fori_loop(0, frames, frame, 0)
    sent_ref[...] = carry[...].astype(BF16)
    hand_out(qbar_ref, qbar_outs)


def tangent_body(groups, count, *refs):
    qd_parts, refs = refs[:groups], refs[groups:]
    sums, firsts, refs = refs[:groups], refs[groups : 2 * groups], refs[2 * groups :]
    gots, refs = refs[:count], refs[count:]
    q_ref, prefix_ref, unit_ref, scale_ref, flow_ref, out_ref, qd_ref, s_ref, dots = refs
    share = q_ref.shape[1]
    frames = prefix_ref.shape[0]
    take_in(qd_parts, qd_ref)
    before = before_of(gots, True)[:, share:]
    prefixes(before, sums, firsts, slice(share, 2 * share), s_ref, dots)

    def frame(f, _):
        tokens = pl.ds(pl.multiple_of(f * SPAN, SPAN), SPAN)
        for s in range(groups):
            outs = []
            for p in range(share // PAIR):
                at = slice(p * PAIR, (p + 1) * PAIR)
                moved = dot(spread(prefix_ref[f, s, :, at].astype(F32)), qd_ref[s, at, tokens])
                moved = moved + dot(spread(dots[f, s, :, at].astype(F32)), q_ref[s, at, tokens])
                for h in range(2):
                    rows = slice(p * PAIR + h * HEAD, p * PAIR + (h + 1) * HEAD)
                    part = moved[h * HEAD : (h + 1) * HEAD]
                    part = part * scale_ref[f, s, 2 * p + h : 2 * p + h + 1, :]
                    unit = unit_ref[f, s, rows, :].astype(F32)
                    along = jnp.sum(unit * part, 0, keepdims=True) * (1.0 / HEAD)
                    outs.append(part - unit * along)
            out_ref[f, s] = jnp.concatenate(outs, 0).T.astype(BF16)
            flow_ref[f, s] = unit_ref[f, s].astype(F32).T.astype(BF16)
        return 0

    lax.fori_loop(0, frames, frame, 0)


def back_body(count, suffix_ref, *refs):
    gots, refs = refs[:count], refs[count:]
    *outs, after_ref = refs
    after = before_of(gots, False)
    after_ref[...] = after
    for k, out_ref in enumerate(outs):
        out_ref[...] = (suffix_ref[mine() ^ k] + after).astype(BF16)


def cotangent_body(suffix_ref, after_ref, out_ref):
    tiles, frames = suffix_ref.shape[:2]
    for f in range(frames):
        for s in range(tiles):
            for h in range(out_ref.shape[1]):
                at = slice(h * HEAD, (h + 1) * HEAD)
                out_ref[f * tiles + s, h] = suffix_ref[s, f, :, at] + after_ref[:, at]


def adjoint_query_body(w_ref, *refs):
    *parts, out_ref, held = refs
    take_in(parts, held)
    out_ref[...] = dot(w_ref[...], held[...].reshape(-1, held.shape[2]))


def adjoint_body(groups, *refs):
    s_parts, refs = refs[:groups], refs[groups:]
    both, part_ref, k_ref, v_ref, out_ref, bars, state_ref = refs
    take_in(s_parts, state_ref)
    _, frames, _, share = state_ref.shape

    def group(g, _):
        for half in range(share // PAIR):
            rows = pl.ds(pl.multiple_of(g * share + half * PAIR, 16), PAIR)
            for f in range(frames):
                at = slice(f * SPAN, (f + 1) * SPAN)
                state = spread(state_ref[g, f, :, half * PAIR : (half + 1) * PAIR].astype(F32))
                bars[0, rows, at] = dot(state, both[1, rows, at]).astype(BF16)
                bars[1, rows, at] = dot_tn(state, both[0, rows, at]).astype(BF16)
        return 0

    lax.fori_loop(0, groups, group, 0)
    out = part_ref[...] + dot(k_ref[...], bars[0]) + dot(v_ref[...], bars[1])
    out_ref[...] = out.T.astype(BF16)


def scan_over(total, sent, axis, forward):
    size = lax.axis_size(axis)
    assert size % 2 == 0
    gots = [lax.ppermute(sent, axis, [(i, i ^ 1) for i in range(size)])]
    total = total + gots[0].astype(F32)
    shifts = [2 * k for k in range(1, size // 2)]
    if len(shifts) > 3:
        shifts = [2 << k for k in range(len(shifts).bit_length())]
    paired = total.astype(BF16)
    for by in shifts:
        pairs = [(i, i + by) for i in range(size - by)]
        if not forward:
            pairs = [(j, i) for i, j in pairs]
        gots.append(lax.ppermute(paired, axis, pairs))
        if size > 8:
            total = total + gots[-1].astype(F32)
            paired = total.astype(BF16)
    return gots


def on_device(
    video, conv_weight, embed_weight, q_weight, k_weight, v_weight, initial_state, probe_in, probe_out
):
    groups, tms = lax.axis_size("space"), lax.axis_size("tm")
    frames, tile_rows, columns, channels = video.shape
    assert tile_rows * columns == SPAN
    tokens = frames * SPAN
    share = D // groups
    heads = HEADS // groups

    first, last = video[:, :1], video[:, -1:]
    up = [(i, i + 1) for i in range(groups - 1)]
    down = [(j, i) for i, j in up]
    above = lax.ppermute(last, "space", up)
    below = lax.ppermute(first, "space", down)

    taps = conv_weight.reshape(3, 9 * channels, -1)
    weight_bytes = 2 * D * D

    def conv(source, target, main, dtype):
        return call(
            functools.partial(conv_body, source, target),
            [struct((tokens, taps.shape[2]), dtype)], (video, above, below, main, two_taps),
            scratch=[pltpu.VMEM((tokens, taps.shape[1]), BF16)],
            flops=27 * tokens * channels * channels, moved=taps.size + 6 * video.size,
        )[0]

    two_tall = (2, D, tokens)
    part = struct((share, tokens), BF16)
    grouped = (groups, share, tokens)
    held = pltpu.VMEM(grouped, BF16)

    *query_dot, direction, q_near, two_taps = call(
        probe_body,
        [part] * groups
        + [struct((tokens, D), BF16), struct(q_weight.shape, BF16), struct((2,) + taps.shape[1:], BF16)],
        (probe_in.reshape(tokens, D), q_weight, taps), far=3,
        scratch=[pltpu.VMEM((tokens, D), jnp.int32), held, pltpu.SemaphoreType.DMA((3,))],
        flops=2 * tokens * D * D, moved=weight_bytes + 8 * tokens * D,
    )
    query_dot = exchange(query_dot)

    far = conv(1, 0, two_taps, BF16)
    far = lax.ppermute(far, "tm", [(t, t + 1) for t in range(tms - 1)])
    dots, last_tap = call(
        probe_pair_body, [struct(two_tall, BF16), struct(taps.shape[1:], BF16)],
        (taps, direction, k_weight, v_weight), far=1, scratch=[pltpu.SemaphoreType.DMA],
        flops=4 * tokens * D * D, moved=2 * weight_bytes + 6 * tokens * D,
    )
    near = conv(0, 1, last_tap, F32)

    assert frames == 2
    state_part = struct((HEAD, 2 * share), BF16)
    latent, both, *states = call(
        state_body,
        [struct((tokens, D), BF16), struct(two_tall, BF16)] + [state_part] * (2 * groups),
        (near, far, embed_weight, dots, k_weight, v_weight),
        scratch=[pltpu.VMEM((2, groups) + state_part.shape, BF16)],
        flops=4 * tokens * D * D, moved=2 * weight_bytes + 14 * tokens * D,
    )
    sums, firsts = exchange(states[:groups]), states[groups:]

    query = call(
        query_body, [part] * groups, (latent, q_near), scratch=[held],
        flops=2 * tokens * D * D, moved=weight_bytes + 4 * tokens * D,
    )
    total, sent = call(
        total_body,
        [struct((HEAD, 2 * share), F32), struct((HEAD, 2 * share), BF16)], sums,
        moved=8 * HEAD * share * groups,
    )
    query = exchange(query)
    firsts = exchange(firsts)
    gots = scan_over(total, sent, "tm", True)

    shape_fs = (frames, groups, SPAN, share)
    flip_fs = (frames, groups, share, SPAN)
    cotangent = call(
        flip_body, [struct(flip_fs, BF16)], (probe_out.reshape(shape_fs), sent),
        moved=6 * tokens * D,
    )[0]

    prefix_shape = (frames, groups, HEAD, share)
    state_held = pltpu.VMEM(prefix_shape, F32)
    *query_bar, query, unit, scale, suffix, bar_sent, prefix = call(
        functools.partial(flow_body, groups, len(gots)),
        [part] * groups
        + [
            struct(grouped, BF16),
            struct(flip_fs, BF16),
            struct((frames, groups, heads, SPAN), F32),
            struct((groups, frames, HEAD, share), F32),
            struct((HEAD, share), BF16),
            struct(prefix_shape, BF16),
        ],
        (*query, *sums, *firsts, *gots, initial_state, cotangent),
        scratch=[pltpu.VMEM((HEAD, share), F32), state_held, pltpu.VMEM((HEAD, share), F32), held],
        flops=12 * tokens * D * PAIR, moved=10 * tokens * D,
    )
    query_bar = exchange(query_bar)
    bar_gots = scan_over(suffix[0, 0], bar_sent, "tm", False)

    flow, tangent = call(
        functools.partial(tangent_body, groups, len(gots)), [struct(shape_fs, BF16)] * 2,
        (*query_dot, *sums, *firsts, *gots, query, prefix, unit, scale),
        scratch=[held, state_held, pltpu.VMEM(prefix_shape, BF16)],
        flops=12 * tokens * D * PAIR, moved=10 * tokens * D,
    )

    *state_back, after = call(
        functools.partial(back_body, len(bar_gots)),
        [struct((frames, HEAD, share), BF16)] * groups + [struct((HEAD, share), F32)],
        (suffix, *bar_gots), moved=10 * frames * groups * HEAD * share,
    )
    state_back, flow, tangent = lax.optimization_barrier((state_back, flow, tangent))
    state_back = exchange(state_back)
    state_bar = call(
        cotangent_body, [struct((frames * groups, heads, HEAD, HEAD), F32)],
        (suffix, after), moved=10 * frames * groups * HEAD * share,
    )[0]
    query_part = call(
        adjoint_query_body, [struct((D, tokens), F32)], (q_near, *query_bar),
        scratch=[held], flops=2 * tokens * D * D, moved=weight_bytes + 6 * tokens * D,
    )[0]
    adjoint = call(
        functools.partial(adjoint_body, groups), [struct((tokens, D), BF16)],
        (*state_back, both, query_part, k_weight, v_weight),
        scratch=[pltpu.VMEM(two_tall, BF16), pltpu.VMEM((groups, frames, HEAD, share), BF16)],
        flops=4 * tokens * D * D, moved=2 * weight_bytes + 10 * tokens * D,
    )[0]
    out_shape = (frames, groups * tile_rows, columns, share)
    return (
        flow.reshape(out_shape),
        tangent.reshape(out_shape),
        adjoint.reshape(frames, tile_rows, columns, D),
        state_bar,
    )


def solution(mesh):
    in_specs = (
        P("tm", "space", None, None),
        P(),
        P(),
        P(),
        P(),
        P(),
        P("space", None, None),
        P("tm", "space", None, None),
        P("tm", None, None, "space"),
    )
    out_specs = (
        P("tm", None, None, "space"),
        P("tm", None, None, "space"),
        P("tm", "space", None, None),
        P("tm", "space", None, None),
    )
    return jax.shard_map(
        on_device, mesh=mesh, in_specs=in_specs, out_specs=out_specs, check_vma=False
    )
```

```python
import functools

import jax
import jax.numpy as jnp
from jax import lax
from jax.experimental import pallas as pl
from jax.experimental.pallas import tpu as pltpu
from jax.sharding import PartitionSpec as P


D = 1152
HEADS = 16
SPAN = 256
HEAD = D // HEADS
PAIR = 2 * HEAD
F32 = jnp.float32
BF16 = jnp.bfloat16
VMEM_BYTES = 14 * 1024 * 1024


def call(body, outs, args, scratch=(), flops=0, moved=0, far=0):
    vmem = pl.BlockSpec(memory_space=pltpu.VMEM)
    anywhere = pl.BlockSpec(memory_space=pltpu.HBM)
    args = [pltpu.with_memory_space_constraint(a, pltpu.HBM) for a in args[:far]] + list(args[far:])
    return pl.pallas_call(
        body,
        in_specs=[anywhere] * far + [vmem] * (len(args) - far),
        out_specs=[vmem] * len(outs),
        out_shape=outs,
        scratch_shapes=list(scratch),
        compiler_params=pltpu.CompilerParams(vmem_limit_bytes=VMEM_BYTES),
        cost_estimate=pl.CostEstimate(flops=flops, bytes_accessed=moved, transcendentals=0),
    )(*args)


def struct(shape, dtype):
    return jax.ShapeDtypeStruct(shape, dtype)


def dot(a, b):
    return jnp.dot(a, b, preferred_element_type=F32)


def dot_nt(a, b):
    return lax.dot_general(a, b, (((1,), (1,)), ((), ())), preferred_element_type=F32)


def dot_tn(a, b):
    return lax.dot_general(a, b, (((0,), (0,)), ((), ())), preferred_element_type=F32)


def same_head():
    row = lax.broadcasted_iota(jnp.int32, (PAIR, PAIR), 0) < HEAD
    col = lax.broadcasted_iota(jnp.int32, (PAIR, PAIR), 1) < HEAD
    return row == col


def spread(packed):
    both = jnp.concatenate([packed, packed], 0)
    return jnp.where(same_head(), both, 0.0).astype(BF16)


def packed_of(square):
    col = lax.broadcasted_iota(jnp.int32, (HEAD, PAIR), 1) < HEAD
    return jnp.where(col, square[:HEAD], square[HEAD:])


def project(x, w):
    return dot(x, w).T.astype(BF16)


def mine():
    return lax.axis_index("space")


def hand_out(held, outs):
    for k, out_ref in enumerate(outs):
        out_ref[...] = held[mine() ^ k]


def take_in(parts, held):
    for k, part_ref in enumerate(parts):
        held[mine() ^ k] = part_ref[...]


def exchange(parts):
    size = lax.axis_size("space")
    got = [parts[0]]
    for k in range(1, size):
        got.append(lax.ppermute(parts[k], "space", [(i, i ^ k) for i in range(size)]))
    return got


def project_groups(x, w_ref, held):
    held[...] = project(x, w_ref[...]).reshape(held.shape)


def probe_body(x_hbm, w_hbm, taps_hbm, *rest):
    *outs, x_out, w_ref, taps_ref, x_ref, held, sems = rest
    copies = [
        pltpu.make_async_copy(source, target, sems.at[i])
        for i, (source, target) in enumerate(
            ((x_hbm, x_ref), (w_hbm, w_ref), (taps_hbm.at[pl.ds(0, 2)], taps_ref))
        )
    ]
    copies[0].start()
    copies[1].start()
    copies[0].wait()
    x_out[...] = x_ref[...].astype(F32).astype(BF16)
    copies[1].wait()
    copies[2].start()
    project_groups(x_out[...], w_ref, held)
    hand_out(held, outs)
    copies[2].wait()


def query_body(x_ref, w_ref, *rest):
    *outs, held = rest
    project_groups(x_ref[...], w_ref, held)
    hand_out(held, outs)


def probe_pair_body(taps_hbm, x_ref, k_ref, v_ref, out_ref, taps_ref, sem):
    copy = pltpu.make_async_copy(taps_hbm.at[2], taps_ref, sem)
    copy.start()
    out_ref[0] = project(x_ref[...], k_ref[...])
    out_ref[1] = project(x_ref[...], v_ref[...])
    copy.wait()


def flip_body(po_ref, tie_ref, out_ref):
    frames, tiles = po_ref.shape[:2]

    def flip(i, _):
        f, s = i // tiles, i % tiles
        out_ref[f, s] = po_ref[f, s].astype(F32).T.astype(BF16)
        return 0

    lax.fori_loop(0, frames * tiles, flip, 0)


def conv_body(source, target, own_ref, up_ref, down_ref, main_ref, mid_ref, out_ref, wide):
    frames, tile_rows, columns, channels = own_ref.shape
    tokens = tile_rows * columns
    span = (tile_rows + 2) * columns
    column = lax.broadcasted_iota(jnp.int32, (span, channels), 0) % columns
    for f in range(frames):
        mid, top, bottom = (r[f].reshape(-1, channels) for r in (own_ref, up_ref, down_ref))
        x = jnp.concatenate([top, mid, bottom], 0).astype(F32)
        left = jnp.where(column == 0, 0.0, pltpu.roll(x, 1, 0))
        right = jnp.where(column == columns - 1, 0.0, pltpu.roll(x, span - 1, 0))
        for n, part in enumerate((left, x, right)):
            part = part.astype(BF16)
            for b in range(3):
                at = (3 * b + n) * channels
                wide[f * tokens : (f + 1) * tokens, at : at + channels] = part[
                    b * columns : b * columns + tokens
                ]
    total = dot(wide[...], main_ref[...] if len(main_ref.shape) == 2 else main_ref[0])
    extra = dot(wide[source * tokens : (source + 1) * tokens, :], mid_ref[1])
    for f in range(frames):
        part = total[f * tokens : (f + 1) * tokens]
        part = part + extra if f == target else part
        out_ref[f * tokens : (f + 1) * tokens, :] = part.astype(out_ref.dtype)


def state_body(near_ref, far_ref, embed_ref, dots, k_ref, v_ref, latent, both, *rest):
    *outs, state_ref, first_ref = rest
    groups = state_ref.shape[0]
    u = near_ref[...] + far_ref[...].astype(F32)
    active = (u / (1.0 + jnp.exp(-u))).astype(BF16)
    latent[...] = dot(active, embed_ref[...]).astype(BF16)
    both[0] = project(latent[...], k_ref[...])
    both[1] = project(latent[...], v_ref[...])
    share = state_ref.shape[2] // 2

    def group(g, _):
        for half in range(share // PAIR):
            rows = pl.ds(pl.multiple_of(g * share + half * PAIR, 16), PAIR)
            blocks = []
            for f in range(2):
                at = slice(f * SPAN, (f + 1) * SPAN)
                kt, vt = both[0, rows, at], both[1, rows, at]
                state = dot_nt(vt, kt)
                moved = dot_nt(vt, dots[0, rows, at]) + dot_nt(dots[1, rows, at], kt)
                blocks.append((packed_of(state), packed_of(moved)))
            for kind in range(2):
                to = kind * share + half * PAIR
                first, second = blocks[0][kind], blocks[1][kind]
                state_ref[g, :, to : to + PAIR] = (first + second).astype(BF16)
                to = half * PAIR
                first_ref[kind, g, :, to : to + PAIR] = first.astype(BF16)
        return 0

    lax.fori_loop(0, groups, group, 0)
    hand_out(state_ref, outs[:groups])
    hand_out(first_ref.at[0], outs[groups : 2 * groups])
    hand_out(first_ref.at[1], outs[2 * groups :])


def total_body(*refs):
    *parts, out_ref, sent_ref = refs
    total = sum(part[...].astype(F32) for part in parts)
    out_ref[...] = total
    sent_ref[...] = total.astype(BF16)


def prefixes(start, sums, firsts, at, held, out_ref):
    groups = len(sums)
    for k in range(groups):
        first = firsts[k][...].astype(F32)
        held[0, mine() ^ k] = first
        held[1, mine() ^ k] = sums[k][:, at].astype(F32) - first
    for f in range(2):
        for s in range(groups):
            start = start + held[f, s]
            out_ref[f, s] = start.astype(BF16)


def partners(size):
    assert size & (size - 1) == 0
    return [1, 2, 4, 6][: max(size // 2, 1)] if size <= 8 else [1 << k for k in range(size.bit_length() - 1)]


def before_of(gots, forward):
    place = lax.axis_index("tm")
    total = 0.0
    for by, got in zip(partners(lax.axis_size("tm")), gots):
        other = place ^ by
        counts = other < place if forward else other > place
        total = total + jnp.where(counts, got[...].astype(F32), 0.0)
    return total


def flow_body(groups, count, *refs):
    q_parts, refs = refs[:groups], refs[groups:]
    sums, firsts, refs = refs[:groups], refs[groups : 2 * groups], refs[2 * groups :]
    gots, refs = refs[:count], refs[count:]
    init_ref, po_ref, *refs = refs
    qbar_outs, refs = refs[:groups], refs[groups:]
    unit_ref, scale_ref, suffix_ref, sent_ref, prefix_ref, held, s_ref, pbar_ref = refs
    share = held.shape[1]
    frames = prefix_ref.shape[0]
    for h in range(init_ref.shape[0]):
        held[:, h * HEAD : (h + 1) * HEAD] = init_ref[h]
    before = before_of(gots, True)[:, :share]
    for p in range(share // PAIR):
        at = slice(p * PAIR, (p + 1) * PAIR)
        packed = held[:, at]
        square = jnp.where(same_head(), jnp.concatenate([packed, packed], 0), 0.0)
        held[:, at] = packed_of(square.T) + before[:, at]
    prefixes(held[...], sums, firsts, slice(0, share), s_ref, prefix_ref)

    def frame(f, _):
        tokens = pl.ds(pl.multiple_of(f * SPAN, SPAN), SPAN)
        for k in range(groups):
            s = mine() ^ k
            for p in range(share // PAIR):
                at = slice(p * PAIR, (p + 1) * PAIR)
                query = q_parts[k][at, tokens]
                prefix = spread(prefix_ref[f, s, :, at].astype(F32))
                mixed = dot(prefix, query)
                bars = []
                for h in range(2):
                    rows = slice(p * PAIR + h * HEAD, p * PAIR + (h + 1) * HEAD)
                    part = mixed[h * HEAD : (h + 1) * HEAD]
                    scale = lax.rsqrt(jnp.sum(part * part, 0, keepdims=True) * (1.0 / HEAD) + 1e-6)
                    unit = part * scale
                    cotangent = po_ref[f, s, rows, :].astype(F32)
                    across = jnp.sum(unit * cotangent, 0, keepdims=True) * (1.0 / HEAD)
                    bars.append((cotangent - unit * across) * scale)
                    unit_ref[f, s, rows, :] = unit.astype(BF16)
                    scale_ref[f, s, 2 * p + h : 2 * p + h + 1, :] = scale
                mixed_bar = jnp.concatenate(bars, 0).astype(BF16)
                pbar_ref[f, s, :, at] = packed_of(dot_nt(query, mixed_bar))
                qbar_outs[k][at, tokens] = dot_tn(prefix, mixed_bar).astype(BF16)
        return 0

    lax.fori_loop(0, frames, frame, 0)
    carry = jnp.zeros(held.shape, F32)
    for f in reversed(range(frames)):
        for s in reversed(range(groups)):
            carry = carry + pbar_ref[f, s]
            suffix_ref[s, f] = carry
    sent_ref[...] = carry.astype(BF16)


def tangent_body(groups, count, *refs):
    qd_parts, q_parts, refs = refs[:groups], refs[groups : 2 * groups], refs[2 * groups :]
    sums, firsts, refs = refs[:groups], refs[groups : 2 * groups], refs[2 * groups :]
    gots, refs = refs[:count], refs[count:]
    prefix_ref, unit_ref, scale_ref, out_ref, s_ref, dots = refs
    share = prefix_ref.shape[3]
    frames = prefix_ref.shape[0]
    before = before_of(gots, True)[:, share:]
    prefixes(before, sums, firsts, slice(share, 2 * share), s_ref, dots)

    def frame(f, _):
        tokens = pl.ds(pl.multiple_of(f * SPAN, SPAN), SPAN)
        for k in range(groups):
            s = mine() ^ k
            outs = []
            for p in range(share // PAIR):
                at = slice(p * PAIR, (p + 1) * PAIR)
                moved = dot(spread(prefix_ref[f, s, :, at].astype(F32)), qd_parts[k][at, tokens])
                moved = moved + dot(spread(dots[f, s, :, at].astype(F32)), q_parts[k][at, tokens])
                for h in range(2):
                    rows = slice(p * PAIR + h * HEAD, p * PAIR + (h + 1) * HEAD)
                    part = moved[h * HEAD : (h + 1) * HEAD]
                    part = part * scale_ref[f, s, 2 * p + h : 2 * p + h + 1, :]
                    unit = unit_ref[f, s, rows, :].astype(F32)
                    along = jnp.sum(unit * part, 0, keepdims=True) * (1.0 / HEAD)
                    outs.append(part - unit * along)
            out_ref[f, s] = jnp.concatenate(outs, 0).T.astype(BF16)
        return 0

    lax.fori_loop(0, frames, frame, 0)


def unit_out_body(unit_ref, out_ref):
    frames, groups = unit_ref.shape[:2]

    def block(i, _):
        f, s = i // groups, i % groups
        out_ref[f, s] = unit_ref[f, s].astype(F32).T.astype(BF16)
        return 0

    lax.fori_loop(0, frames * groups, block, 0)


def back_body(count, suffix_ref, *refs):
    gots, refs = refs[:count], refs[count:]
    *outs, after_ref = refs
    after = before_of(gots, False)
    after_ref[...] = after
    for k, out_ref in enumerate(outs):
        out_ref[...] = (suffix_ref[mine() ^ k] + after).astype(BF16)


def cotangent_body(suffix_ref, after_ref, out_ref):
    tiles, frames = suffix_ref.shape[:2]
    for f in range(frames):
        for s in range(tiles):
            for h in range(out_ref.shape[1]):
                at = slice(h * HEAD, (h + 1) * HEAD)
                out_ref[f * tiles + s, h] = suffix_ref[s, f, :, at] + after_ref[:, at]


def adjoint_query_body(w_ref, *refs):
    *parts, out_ref, held = refs
    take_in(parts, held)
    out_ref[...] = dot(w_ref[...], held[...].reshape(-1, held.shape[2]))


def adjoint_body(groups, *refs):
    s_parts, refs = refs[:groups], refs[groups:]
    both, part_ref, k_ref, v_ref, out_ref, bars, state_ref = refs
    take_in(s_parts, state_ref)
    _, frames, _, share = state_ref.shape

    def group(g, _):
        for half in range(share // PAIR):
            rows = pl.ds(pl.multiple_of(g * share + half * PAIR, 16), PAIR)
            for f in range(frames):
                at = slice(f * SPAN, (f + 1) * SPAN)
                state = spread(state_ref[g, f, :, half * PAIR : (half + 1) * PAIR].astype(F32))
                bars[0, rows, at] = dot(state, both[1, rows, at]).astype(BF16)
                bars[1, rows, at] = dot_tn(state, both[0, rows, at]).astype(BF16)
        return 0

    lax.fori_loop(0, groups, group, 0)
    out = part_ref[...] + dot(k_ref[...], bars[0]) + dot(v_ref[...], bars[1])
    out_ref[...] = out.T.astype(BF16)


def scan_over(total, sent, axis):
    size = lax.axis_size(axis)
    gots = []
    for by in partners(size):
        gots.append(lax.ppermute(sent, axis, [(i, i ^ by) for i in range(size)]))
        if by == 1 or size > 8:
            total = total + gots[-1].astype(F32)
            sent = total.astype(BF16)
    return gots


def on_device(
    video, conv_weight, embed_weight, q_weight, k_weight, v_weight, initial_state, probe_in, probe_out
):
    groups, tms = lax.axis_size("space"), lax.axis_size("tm")
    frames, tile_rows, columns, channels = video.shape
    assert tile_rows * columns == SPAN
    tokens = frames * SPAN
    share = D // groups
    heads = HEADS // groups

    first, last = video[:, :1], video[:, -1:]
    up = [(i, i + 1) for i in range(groups - 1)]
    down = [(j, i) for i, j in up]
    above = lax.ppermute(last, "space", up)
    below = lax.ppermute(first, "space", down)

    taps = conv_weight.reshape(3, 9 * channels, -1)
    weight_bytes = 2 * D * D

    def conv(source, target, main, dtype):
        return call(
            functools.partial(conv_body, source, target),
            [struct((tokens, taps.shape[2]), dtype)], (video, above, below, main, two_taps),
            scratch=[pltpu.VMEM((tokens, taps.shape[1]), BF16)],
            flops=27 * tokens * channels * channels, moved=taps.size + 6 * video.size,
        )[0]

    two_tall = (2, D, tokens)
    part = struct((share, tokens), BF16)
    grouped = (groups, share, tokens)
    held = pltpu.VMEM(grouped, BF16)

    *query_dot, direction, q_near, two_taps = call(
        probe_body,
        [part] * groups
        + [struct((tokens, D), BF16), struct(q_weight.shape, BF16), struct((2,) + taps.shape[1:], BF16)],
        (probe_in.reshape(tokens, D), q_weight, taps), far=3,
        scratch=[pltpu.VMEM((tokens, D), jnp.int32), held, pltpu.SemaphoreType.DMA((3,))],
        flops=2 * tokens * D * D, moved=weight_bytes + 8 * tokens * D,
    )
    query_dot = exchange(query_dot)

    far = conv(1, 0, two_taps, BF16)
    far = lax.ppermute(far, "tm", [(t, t + 1) for t in range(tms - 1)])
    dots, last_tap = call(
        probe_pair_body, [struct(two_tall, BF16), struct(taps.shape[1:], BF16)],
        (taps, direction, k_weight, v_weight), far=1, scratch=[pltpu.SemaphoreType.DMA],
        flops=4 * tokens * D * D, moved=2 * weight_bytes + 6 * tokens * D,
    )
    near = conv(0, 1, last_tap, F32)

    assert frames == 2
    state_part = struct((HEAD, 2 * share), BF16)
    latent, both, *states = call(
        state_body,
        [struct((tokens, D), BF16), struct(two_tall, BF16)] + [state_part] * groups
        + [struct((HEAD, share), BF16)] * (2 * groups),
        (near, far, embed_weight, dots, k_weight, v_weight),
        scratch=[
            pltpu.VMEM((groups,) + state_part.shape, BF16),
            pltpu.VMEM((2, groups, HEAD, share), BF16),
        ],
        flops=4 * tokens * D * D, moved=2 * weight_bytes + 14 * tokens * D,
    )
    sums, firsts = exchange(states[:groups]), states[groups : 2 * groups]
    first_dots = states[2 * groups :]

    query = call(
        query_body, [part] * groups, (latent, q_near), scratch=[held],
        flops=2 * tokens * D * D, moved=weight_bytes + 4 * tokens * D,
    )
    total, sent = call(
        total_body,
        [struct((HEAD, 2 * share), F32), struct((HEAD, 2 * share), BF16)], sums,
        moved=8 * HEAD * share * groups,
    )
    query = exchange(query)
    firsts = exchange(firsts)
    first_dots = exchange(first_dots)
    gots = scan_over(total, sent, "tm")

    shape_fs = (frames, groups, SPAN, share)
    flip_fs = (frames, groups, share, SPAN)
    cotangent = call(
        flip_body, [struct(flip_fs, BF16)], (probe_out.reshape(shape_fs), sent),
        moved=6 * tokens * D,
    )[0]

    prefix_shape = (frames, groups, HEAD, share)
    state_held = pltpu.VMEM(prefix_shape, F32)
    *query_bar, unit, scale, suffix, bar_sent, prefix = call(
        functools.partial(flow_body, groups, len(gots)),
        [part] * groups
        + [
            struct(flip_fs, BF16),
            struct((frames, groups, heads, SPAN), F32),
            struct((groups, frames, HEAD, share), F32),
            struct((HEAD, share), BF16),
            struct(prefix_shape, BF16),
        ],
        (*query, *sums, *firsts, *gots, initial_state, cotangent),
        scratch=[pltpu.VMEM((HEAD, share), F32), state_held, state_held],
        flops=12 * tokens * D * PAIR, moved=10 * tokens * D,
    )
    query_bar = exchange(query_bar)
    bar_gots = scan_over(suffix[0, 0], bar_sent, "tm")

    tangent = call(
        functools.partial(tangent_body, groups, len(gots)), [struct(shape_fs, BF16)],
        (*query_dot, *query, *sums, *first_dots, *gots, prefix, unit, scale),
        scratch=[state_held, pltpu.VMEM(prefix_shape, BF16)],
        flops=12 * tokens * D * PAIR, moved=10 * tokens * D,
    )[0]
    flow = call(unit_out_body, [struct(shape_fs, BF16)], (unit,), moved=4 * tokens * D)[0]

    *state_back, after = call(
        functools.partial(back_body, len(bar_gots)),
        [struct((frames, HEAD, share), BF16)] * groups + [struct((HEAD, share), F32)],
        (suffix, *bar_gots), moved=10 * frames * groups * HEAD * share,
    )
    state_back, tangent = lax.optimization_barrier((state_back, tangent))
    state_back = exchange(state_back)
    state_bar = call(
        cotangent_body, [struct((frames * groups, heads, HEAD, HEAD), F32)],
        (suffix, after), moved=10 * frames * groups * HEAD * share,
    )[0]
    query_part = call(
        adjoint_query_body, [struct((D, tokens), F32)], (q_near, *query_bar),
        scratch=[held], flops=2 * tokens * D * D, moved=weight_bytes + 6 * tokens * D,
    )[0]
    adjoint = call(
        functools.partial(adjoint_body, groups), [struct((tokens, D), BF16)],
        (*state_back, both, query_part, k_weight, v_weight),
        scratch=[pltpu.VMEM(two_tall, BF16), pltpu.VMEM((groups, frames, HEAD, share), BF16)],
        flops=4 * tokens * D * D, moved=2 * weight_bytes + 10 * tokens * D,
    )[0]
    out_shape = (frames, groups * tile_rows, columns, share)
    return (
        flow.reshape(out_shape),
        tangent.reshape(out_shape),
        adjoint.reshape(frames, tile_rows, columns, D),
        state_bar,
    )


def solution(mesh):
    in_specs = (
        P("tm", "space", None, None),
        P(),
        P(),
        P(),
        P(),
        P(),
        P("space", None, None),
        P("tm", "space", None, None),
        P("tm", None, None, "space"),
    )
    out_specs = (
        P("tm", None, None, "space"),
        P("tm", None, None, "space"),
        P("tm", "space", None, None),
        P("tm", "space", None, None),
    )
    return jax.shard_map(
        on_device, mesh=mesh, in_specs=in_specs, out_specs=out_specs, check_vma=False
    )
```

```python
import functools

import jax
import jax.numpy as jnp
from jax import lax
from jax.experimental import pallas as pl
from jax.experimental.pallas import tpu as pltpu
from jax.sharding import PartitionSpec as P


D = 1152
HEADS = 16
SPAN = 256
HEAD = D // HEADS
PAIR = 2 * HEAD
F32 = jnp.float32
BF16 = jnp.bfloat16
VMEM_BYTES = 14 * 1024 * 1024


def call(body, outs, args, scratch=(), flops=0, moved=0, far=0):
    vmem = pl.BlockSpec(memory_space=pltpu.VMEM)
    anywhere = pl.BlockSpec(memory_space=pltpu.HBM)
    args = [pltpu.with_memory_space_constraint(a, pltpu.HBM) for a in args[:far]] + list(args[far:])
    return pl.pallas_call(
        body,
        in_specs=[anywhere] * far + [vmem] * (len(args) - far),
        out_specs=[vmem] * len(outs),
        out_shape=outs,
        scratch_shapes=list(scratch),
        compiler_params=pltpu.CompilerParams(vmem_limit_bytes=VMEM_BYTES),
        cost_estimate=pl.CostEstimate(flops=flops, bytes_accessed=moved, transcendentals=0),
    )(*args)


def struct(shape, dtype):
    return jax.ShapeDtypeStruct(shape, dtype)


def dot(a, b):
    return jnp.dot(a, b, preferred_element_type=F32)


def dot_nt(a, b):
    return lax.dot_general(a, b, (((1,), (1,)), ((), ())), preferred_element_type=F32)


def dot_tn(a, b):
    return lax.dot_general(a, b, (((0,), (0,)), ((), ())), preferred_element_type=F32)


def same_head():
    row = lax.broadcasted_iota(jnp.int32, (PAIR, PAIR), 0) < HEAD
    col = lax.broadcasted_iota(jnp.int32, (PAIR, PAIR), 1) < HEAD
    return row == col


def spread(packed):
    both = jnp.concatenate([packed, packed], 0)
    return jnp.where(same_head(), both, 0.0).astype(BF16)


def packed_of(square):
    col = lax.broadcasted_iota(jnp.int32, (HEAD, PAIR), 1) < HEAD
    return jnp.where(col, square[:HEAD], square[HEAD:])


def project(x, w):
    return dot(x, w).T.astype(BF16)


def mine():
    return lax.axis_index("space")


def hand_out(held, outs):
    for k, out_ref in enumerate(outs):
        out_ref[...] = held[mine() ^ k]


def take_in(parts, held):
    for k, part_ref in enumerate(parts):
        held[mine() ^ k] = part_ref[...]


def exchange(parts):
    size = lax.axis_size("space")
    got = [parts[0]]
    for k in range(1, size):
        got.append(lax.ppermute(parts[k], "space", [(i, i ^ k) for i in range(size)]))
    return got


def project_groups(x, w_ref, held):
    held[...] = project(x, w_ref[...]).reshape(held.shape)


def probe_body(x_hbm, w_hbm, k_hbm, taps_hbm, *rest):
    *outs, x_out, w_ref, k_ref, key_ref, taps_ref, x_ref, held, sems = rest
    copies = [
        pltpu.make_async_copy(source, target, sems.at[i])
        for i, (source, target) in enumerate(
            (
                (x_hbm, x_ref), (w_hbm, w_ref), (k_hbm, k_ref),
                (taps_hbm.at[pl.ds(0, 2)], taps_ref),
            )
        )
    ]
    copies[0].start()
    copies[1].start()
    copies[0].wait()
    x_out[...] = x_ref[...].astype(F32).astype(BF16)
    copies[1].wait()
    copies[2].start()
    copies[3].start()
    project_groups(x_out[...], w_ref, held)
    hand_out(held, outs)
    copies[2].wait()
    key_ref[...] = project(x_out[...], k_ref[...])
    copies[3].wait()


def query_body(x_ref, w_ref, *rest):
    *outs, held = rest
    project_groups(x_ref[...], w_ref, held)
    hand_out(held, outs)


def probe_pair_body(taps_hbm, x_ref, v_ref, out_ref, taps_ref, sem):
    copy = pltpu.make_async_copy(taps_hbm.at[2], taps_ref, sem)
    copy.start()
    out_ref[...] = project(x_ref[...], v_ref[...])
    copy.wait()


def flip_body(po_ref, tie_ref, out_ref):
    frames, tiles = po_ref.shape[:2]

    def flip(i, _):
        f, s = i // tiles, i % tiles
        out_ref[f, s] = po_ref[f, s].astype(F32).T.astype(BF16)
        return 0

    lax.fori_loop(0, frames * tiles, flip, 0)


def conv_body(source, target, own_ref, up_ref, down_ref, main_ref, mid_ref, out_ref, wide):
    frames, tile_rows, columns, channels = own_ref.shape
    tokens = tile_rows * columns
    span = (tile_rows + 2) * columns
    column = lax.broadcasted_iota(jnp.int32, (span, channels), 0) % columns
    for f in range(frames):
        mid, top, bottom = (r[f].reshape(-1, channels) for r in (own_ref, up_ref, down_ref))
        x = jnp.concatenate([top, mid, bottom], 0).astype(F32)
        left = jnp.where(column == 0, 0.0, pltpu.roll(x, 1, 0))
        right = jnp.where(column == columns - 1, 0.0, pltpu.roll(x, span - 1, 0))
        for n, part in enumerate((left, x, right)):
            part = part.astype(BF16)
            for b in range(3):
                at = (3 * b + n) * channels
                wide[f * tokens : (f + 1) * tokens, at : at + channels] = part[
                    b * columns : b * columns + tokens
                ]
    total = dot(wide[...], main_ref[...] if len(main_ref.shape) == 2 else main_ref[0])
    extra = dot(wide[source * tokens : (source + 1) * tokens, :], mid_ref[1])
    for f in range(frames):
        part = total[f * tokens : (f + 1) * tokens]
        part = part + extra if f == target else part
        out_ref[f * tokens : (f + 1) * tokens, :] = part.astype(out_ref.dtype)


def state_body(near_ref, far_ref, embed_ref, key_dots, value_dots, k_ref, v_ref, latent, both, *rest):
    *outs, state_ref, first_ref = rest
    groups = state_ref.shape[0]
    u = near_ref[...] + far_ref[...].astype(F32)
    active = (u / (1.0 + jnp.exp(-u))).astype(BF16)
    latent[...] = dot(active, embed_ref[...]).astype(BF16)
    both[0] = project(latent[...], k_ref[...])
    both[1] = project(latent[...], v_ref[...])
    share = state_ref.shape[2] // 2

    def group(g, _):
        for half in range(share // PAIR):
            rows = pl.ds(pl.multiple_of(g * share + half * PAIR, 16), PAIR)
            blocks = []
            for f in range(2):
                at = slice(f * SPAN, (f + 1) * SPAN)
                kt, vt = both[0, rows, at], both[1, rows, at]
                state = dot_nt(vt, kt)
                moved = dot_nt(vt, key_dots[rows, at]) + dot_nt(value_dots[rows, at], kt)
                blocks.append((packed_of(state), packed_of(moved)))
            for kind in range(2):
                to = kind * share + half * PAIR
                first, second = blocks[0][kind], blocks[1][kind]
                state_ref[g, :, to : to + PAIR] = (first + second).astype(BF16)
                to = half * PAIR
                first_ref[kind, g, :, to : to + PAIR] = first.astype(BF16)
        return 0

    lax.fori_loop(0, groups, group, 0)
    hand_out(state_ref, outs[:groups])
    hand_out(first_ref.at[0], outs[groups : 2 * groups])
    hand_out(first_ref.at[1], outs[2 * groups :])


def total_body(*refs):
    *parts, out_ref, sent_ref = refs
    total = sum(part[...].astype(F32) for part in parts)
    out_ref[...] = total
    sent_ref[...] = total.astype(BF16)


def prefixes(start, sums, firsts, at, held, out_ref):
    groups = len(sums)
    for k in range(groups):
        first = firsts[k][...].astype(F32)
        held[0, mine() ^ k] = first
        held[1, mine() ^ k] = sums[k][:, at].astype(F32) - first
    for f in range(2):
        for s in range(groups):
            start = start + held[f, s]
            out_ref[f, s] = start.astype(BF16)


def partners(size):
    assert size & (size - 1) == 0
    return [1, 2, 4, 6][: max(size // 2, 1)] if size <= 8 else [1 << k for k in range(size.bit_length() - 1)]


def before_of(gots, forward):
    place = lax.axis_index("tm")
    total = 0.0
    for by, got in zip(partners(lax.axis_size("tm")), gots):
        other = place ^ by
        counts = other < place if forward else other > place
        total = total + jnp.where(counts, got[...].astype(F32), 0.0)
    return total


def flow_body(groups, count, *refs):
    q_parts, refs = refs[:groups], refs[groups:]
    sums, firsts, refs = refs[:groups], refs[groups : 2 * groups], refs[2 * groups :]
    gots, refs = refs[:count], refs[count:]
    init_ref, po_ref, *refs = refs
    qbar_outs, refs = refs[:groups], refs[groups:]
    unit_ref, scale_ref, suffix_ref, sent_ref, prefix_ref, held, s_ref, pbar_ref = refs
    share = held.shape[1]
    frames = prefix_ref.shape[0]
    for h in range(init_ref.shape[0]):
        held[:, h * HEAD : (h + 1) * HEAD] = init_ref[h]
    before = before_of(gots, True)[:, :share]
    for p in range(share // PAIR):
        at = slice(p * PAIR, (p + 1) * PAIR)
        packed = held[:, at]
        square = jnp.where(same_head(), jnp.concatenate([packed, packed], 0), 0.0)
        held[:, at] = packed_of(square.T) + before[:, at]
    prefixes(held[...], sums, firsts, slice(0, share), s_ref, prefix_ref)

    def frame(f, _):
        tokens = pl.ds(pl.multiple_of(f * SPAN, SPAN), SPAN)
        for k in range(groups):
            s = mine() ^ k
            for p in range(share // PAIR):
                at = slice(p * PAIR, (p + 1) * PAIR)
                query = q_parts[k][at, tokens]
                prefix = spread(prefix_ref[f, s, :, at].astype(F32))
                mixed = dot(prefix, query)
                bars = []
                for h in range(2):
                    rows = slice(p * PAIR + h * HEAD, p * PAIR + (h + 1) * HEAD)
                    part = mixed[h * HEAD : (h + 1) * HEAD]
                    scale = lax.rsqrt(jnp.sum(part * part, 0, keepdims=True) * (1.0 / HEAD) + 1e-6)
                    unit = part * scale
                    cotangent = po_ref[f, s, rows, :].astype(F32)
                    across = jnp.sum(unit * cotangent, 0, keepdims=True) * (1.0 / HEAD)
                    bars.append((cotangent - unit * across) * scale)
                    unit_ref[f, s, rows, :] = unit.astype(BF16)
                    scale_ref[f, s, 2 * p + h : 2 * p + h + 1, :] = scale
                mixed_bar = jnp.concatenate(bars, 0).astype(BF16)
                pbar_ref[f, s, :, at] = packed_of(dot_nt(query, mixed_bar))
                qbar_outs[k][at, tokens] = dot_tn(prefix, mixed_bar).astype(BF16)
        return 0

    lax.fori_loop(0, frames, frame, 0)
    carry = jnp.zeros(held.shape, F32)
    for f in reversed(range(frames)):
        for s in reversed(range(groups)):
            carry = carry + pbar_ref[f, s]
            suffix_ref[s, f] = carry
    sent_ref[...] = carry.astype(BF16)


def tangent_body(groups, count, *refs):
    qd_parts, q_parts, refs = refs[:groups], refs[groups : 2 * groups], refs[2 * groups :]
    sums, firsts, refs = refs[:groups], refs[groups : 2 * groups], refs[2 * groups :]
    gots, refs = refs[:count], refs[count:]
    prefix_ref, unit_ref, scale_ref, out_ref, s_ref, dots = refs
    share = prefix_ref.shape[3]
    frames = prefix_ref.shape[0]
    before = before_of(gots, True)[:, share:]
    prefixes(before, sums, firsts, slice(share, 2 * share), s_ref, dots)

    def frame(f, _):
        tokens = pl.ds(pl.multiple_of(f * SPAN, SPAN), SPAN)
        for k in range(groups):
            s = mine() ^ k
            outs = []
            for p in range(share // PAIR):
                at = slice(p * PAIR, (p + 1) * PAIR)
                moved = dot(spread(prefix_ref[f, s, :, at].astype(F32)), qd_parts[k][at, tokens])
                moved = moved + dot(spread(dots[f, s, :, at].astype(F32)), q_parts[k][at, tokens])
                for h in range(2):
                    rows = slice(p * PAIR + h * HEAD, p * PAIR + (h + 1) * HEAD)
                    part = moved[h * HEAD : (h + 1) * HEAD]
                    part = part * scale_ref[f, s, 2 * p + h : 2 * p + h + 1, :]
                    unit = unit_ref[f, s, rows, :].astype(F32)
                    along = jnp.sum(unit * part, 0, keepdims=True) * (1.0 / HEAD)
                    outs.append(part - unit * along)
            out_ref[f, s] = jnp.concatenate(outs, 0).T.astype(BF16)
        return 0

    lax.fori_loop(0, frames, frame, 0)


def unit_out_body(unit_ref, out_ref):
    frames, groups = unit_ref.shape[:2]

    def block(i, _):
        f, s = i // groups, i % groups
        out_ref[f, s] = unit_ref[f, s].astype(F32).T.astype(BF16)
        return 0

    lax.fori_loop(0, frames * groups, block, 0)


def back_body(count, suffix_ref, *refs):
    gots, refs = refs[:count], refs[count:]
    *outs, after_ref = refs
    after = before_of(gots, False)
    after_ref[...] = after
    for k, out_ref in enumerate(outs):
        out_ref[...] = (suffix_ref[mine() ^ k] + after).astype(BF16)


def cotangent_body(suffix_ref, after_ref, out_ref):
    tiles, frames = suffix_ref.shape[:2]
    for f in range(frames):
        for s in range(tiles):
            for h in range(out_ref.shape[1]):
                at = slice(h * HEAD, (h + 1) * HEAD)
                out_ref[f * tiles + s, h] = suffix_ref[s, f, :, at] + after_ref[:, at]


def adjoint_query_body(w_ref, *refs):
    *parts, out_ref, held = refs
    take_in(parts, held)
    out_ref[...] = dot(w_ref[...], held[...].reshape(-1, held.shape[2]))


def adjoint_body(groups, *refs):
    s_parts, refs = refs[:groups], refs[groups:]
    both, part_ref, k_ref, v_ref, out_ref, bars, state_ref = refs
    take_in(s_parts, state_ref)
    _, frames, _, share = state_ref.shape

    def group(g, _):
        for half in range(share // PAIR):
            rows = pl.ds(pl.multiple_of(g * share + half * PAIR, 16), PAIR)
            for f in range(frames):
                at = slice(f * SPAN, (f + 1) * SPAN)
                state = spread(state_ref[g, f, :, half * PAIR : (half + 1) * PAIR].astype(F32))
                bars[0, rows, at] = dot(state, both[1, rows, at]).astype(BF16)
                bars[1, rows, at] = dot_tn(state, both[0, rows, at]).astype(BF16)
        return 0

    lax.fori_loop(0, groups, group, 0)
    out = part_ref[...] + dot(k_ref[...], bars[0]) + dot(v_ref[...], bars[1])
    out_ref[...] = out.T.astype(BF16)


def scan_over(total, sent, axis):
    size = lax.axis_size(axis)
    gots = []
    for by in partners(size):
        gots.append(lax.ppermute(sent, axis, [(i, i ^ by) for i in range(size)]))
        if by == 1 or size > 8:
            total = total + gots[-1].astype(F32)
            sent = total.astype(BF16)
    return gots


def on_device(
    video, conv_weight, embed_weight, q_weight, k_weight, v_weight, initial_state, probe_in, probe_out
):
    groups, tms = lax.axis_size("space"), lax.axis_size("tm")
    frames, tile_rows, columns, channels = video.shape
    assert tile_rows * columns == SPAN
    tokens = frames * SPAN
    share = D // groups
    heads = HEADS // groups

    first, last = video[:, :1], video[:, -1:]
    up = [(i, i + 1) for i in range(groups - 1)]
    down = [(j, i) for i, j in up]
    above = lax.ppermute(last, "space", up)
    below = lax.ppermute(first, "space", down)

    taps = conv_weight.reshape(3, 9 * channels, -1)
    weight_bytes = 2 * D * D

    def conv(source, target, main, dtype):
        return call(
            functools.partial(conv_body, source, target),
            [struct((tokens, taps.shape[2]), dtype)], (video, above, below, main, two_taps),
            scratch=[pltpu.VMEM((tokens, taps.shape[1]), BF16)],
            flops=27 * tokens * channels * channels, moved=taps.size + 6 * video.size,
        )[0]

    two_tall = (2, D, tokens)
    part = struct((share, tokens), BF16)
    grouped = (groups, share, tokens)
    held = pltpu.VMEM(grouped, BF16)

    *query_dot, direction, q_near, k_near, key_dot, two_taps = call(
        probe_body,
        [part] * groups
        + [struct((tokens, D), BF16), struct(q_weight.shape, BF16), struct(k_weight.shape, BF16), struct((D, tokens), BF16), struct((2,) + taps.shape[1:], BF16)],
        (probe_in.reshape(tokens, D), q_weight, k_weight, taps), far=4,
        scratch=[pltpu.VMEM((tokens, D), jnp.int32), held, pltpu.SemaphoreType.DMA((4,))],
        flops=2 * tokens * D * D, moved=weight_bytes + 8 * tokens * D,
    )
    query_dot = exchange(query_dot)

    far = conv(1, 0, two_taps, BF16)
    far = lax.ppermute(far, "tm", [(t, t + 1) for t in range(tms - 1)])
    value_dot, last_tap = call(
        probe_pair_body, [struct((D, tokens), BF16), struct(taps.shape[1:], BF16)],
        (taps, direction, v_weight), far=1, scratch=[pltpu.SemaphoreType.DMA],
        flops=4 * tokens * D * D, moved=2 * weight_bytes + 6 * tokens * D,
    )
    near = conv(0, 1, last_tap, F32)

    assert frames == 2
    state_part = struct((HEAD, 2 * share), BF16)
    latent, both, *states = call(
        state_body,
        [struct((tokens, D), BF16), struct(two_tall, BF16)] + [state_part] * groups
        + [struct((HEAD, share), BF16)] * (2 * groups),
        (near, far, embed_weight, key_dot, value_dot, k_near, v_weight),
        scratch=[
            pltpu.VMEM((groups,) + state_part.shape, BF16),
            pltpu.VMEM((2, groups, HEAD, share), BF16),
        ],
        flops=4 * tokens * D * D, moved=2 * weight_bytes + 14 * tokens * D,
    )
    sums, firsts = exchange(states[:groups]), states[groups : 2 * groups]
    first_dots = states[2 * groups :]

    query = call(
        query_body, [part] * groups, (latent, q_near), scratch=[held],
        flops=2 * tokens * D * D, moved=weight_bytes + 4 * tokens * D,
    )
    total, sent = call(
        total_body,
        [struct((HEAD, 2 * share), F32), struct((HEAD, 2 * share), BF16)], sums,
        moved=8 * HEAD * share * groups,
    )
    query = exchange(query)
    firsts = exchange(firsts)
    first_dots = exchange(first_dots)
    gots = scan_over(total, sent, "tm")

    shape_fs = (frames, groups, SPAN, share)
    flip_fs = (frames, groups, share, SPAN)
    cotangent = call(
        flip_body, [struct(flip_fs, BF16)], (probe_out.reshape(shape_fs), sent),
        moved=6 * tokens * D,
    )[0]

    prefix_shape = (frames, groups, HEAD, share)
    state_held = pltpu.VMEM(prefix_shape, F32)
    *query_bar, unit, scale, suffix, bar_sent, prefix = call(
        functools.partial(flow_body, groups, len(gots)),
        [part] * groups
        + [
            struct(flip_fs, BF16),
            struct((frames, groups, heads, SPAN), F32),
            struct((groups, frames, HEAD, share), F32),
            struct((HEAD, share), BF16),
            struct(prefix_shape, BF16),
        ],
        (*query, *sums, *firsts, *gots, initial_state, cotangent),
        scratch=[pltpu.VMEM((HEAD, share), F32), state_held, state_held],
        flops=12 * tokens * D * PAIR, moved=10 * tokens * D,
    )
    query_bar = exchange(query_bar)
    bar_gots = scan_over(suffix[0, 0], bar_sent, "tm")

    tangent = call(
        functools.partial(tangent_body, groups, len(gots)), [struct(shape_fs, BF16)],
        (*query_dot, *query, *sums, *first_dots, *gots, prefix, unit, scale),
        scratch=[state_held, pltpu.VMEM(prefix_shape, BF16)],
        flops=12 * tokens * D * PAIR, moved=10 * tokens * D,
    )[0]
    flow = call(unit_out_body, [struct(shape_fs, BF16)], (unit,), moved=4 * tokens * D)[0]

    *state_back, after = call(
        functools.partial(back_body, len(bar_gots)),
        [struct((frames, HEAD, share), BF16)] * groups + [struct((HEAD, share), F32)],
        (suffix, *bar_gots), moved=10 * frames * groups * HEAD * share,
    )
    state_back, tangent = lax.optimization_barrier((state_back, tangent))
    state_back = exchange(state_back)
    state_bar = call(
        cotangent_body, [struct((frames * groups, heads, HEAD, HEAD), F32)],
        (suffix, after), moved=10 * frames * groups * HEAD * share,
    )[0]
    query_part = call(
        adjoint_query_body, [struct((D, tokens), F32)], (q_near, *query_bar),
        scratch=[held], flops=2 * tokens * D * D, moved=weight_bytes + 6 * tokens * D,
    )[0]
    adjoint = call(
        functools.partial(adjoint_body, groups), [struct((tokens, D), BF16)],
        (*state_back, both, query_part, k_near, v_weight),
        scratch=[pltpu.VMEM(two_tall, BF16), pltpu.VMEM((groups, frames, HEAD, share), BF16)],
        flops=4 * tokens * D * D, moved=2 * weight_bytes + 10 * tokens * D,
    )[0]
    out_shape = (frames, groups * tile_rows, columns, share)
    return (
        flow.reshape(out_shape),
        tangent.reshape(out_shape),
        adjoint.reshape(frames, tile_rows, columns, D),
        state_bar,
    )


def solution(mesh):
    in_specs = (
        P("tm", "space", None, None),
        P(),
        P(),
        P(),
        P(),
        P(),
        P("space", None, None),
        P("tm", "space", None, None),
        P("tm", None, None, "space"),
    )
    out_specs = (
        P("tm", None, None, "space"),
        P("tm", None, None, "space"),
        P("tm", "space", None, None),
        P("tm", "space", None, None),
    )
    return jax.shard_map(
        on_device, mesh=mesh, in_specs=in_specs, out_specs=out_specs, check_vma=False
    )
```
